128 devices in a mesh: grp: 4 (over z_hi, core), dev: 32 (over z_lo, y, x).
Axes of the slice: x: 4, y: 4, z: 4 (z_hi: 2, z_lo: 2; z = z_hi * 2 + z_lo), core: 2. Of those that a mesh axis runs over, the one named last changes fastest.
Arguments:
- initial_state: float32 [5, 256, 32, 128], P(None, 'dev', 'grp'), may hold values from -6 to 6
- viscosity: float32 [256, 32, 128], P('dev', 'grp'), may hold values from 0.02 to 0.12
- speeds: float32 [5, 3], replicated, may hold values from -0.3 to 0.3
- energy_weights: float32 [5], replicated, may hold values from 0.5 to 2
- block_index: int32 [2, 6], replicated, may hold values from 0 to 7
- block_offset: int32 [2], replicated, may hold values from 0 to 7
Outputs:
- final_state: float32 [5, 256, 32, 128], P(None, 'dev', 'grp')
- modes: bfloat16 [64, 2, 2, 5, 256, 32, 128], P('dev', None, None, None, None, 'grp')
- leading_energy: float32 [64], P('dev')
The draws below stay inside these ranges and needn't reach their ends.
All inputs are finite; a program needn't handle non-finite values.
Results may differ from the reference program's by a relative error of at most 0.0075.
Values may be sent and summed in bfloat16 or wider, within the bound.
No kernel may reach another device: no remote copies, remote signals or barrier semaphores. Data moves between devices by JAX's collectives and lax.ppermute only.
A program may use at most 256 MiB of HBM per device.

```python
import math
import jax
import jax.numpy as jnp
from jax import lax

VARS = 5
FREQS = 64
BLOCKS = 2
SNAPS = 8
BLOCK_LEN = 6
NY = 128
NX = 256
NZ = 32


def set_ends(entries, rng, low, largest):
    index_at = [jax.random.randint(jax.random.fold_in(rng, axis), (), 0, length) for axis, length in enumerate(entries.shape)]
    widest = entries.shape.index(max(entries.shape))
    beside = index_at[:widest] + [(index_at[widest] + 1) % entries.shape[widest]] + index_at[widest + 1:]
    return entries.at[tuple(index_at)].set(low).at[tuple(beside)].set(largest)


def steps_of(rng, dims, split, least, high):
    loudness, own = 1.0, jax.random.fold_in(rng, 6)
    for dim, shards_of in split:
        heights = jnp.exp(jax.random.uniform(jax.random.fold_in(own, dim), (shards_of,), jnp.float32, least / len(split), high / len(split)))
        loudness = loudness * jnp.repeat(heights, dims[dim] // shards_of).reshape([-1 if axis == dim else 1 for axis in range(len(dims))])
    return loudness


def noise(key, dims, scale, most, split=(), held_as=jnp.bfloat16):
    gain = steps_of(key, dims, split, -0.22, 0.18) if split else 1.0
    values = jax.random.normal(key, dims, jnp.float32) * scale * gain
    return jnp.minimum(jnp.maximum(values, -most), most).astype(held_as)


def setup_inputs(seed: int = 0) -> dict:
    arg_keys = jax.random.split(jax.random.key(seed), 7)
    initial_state = noise(arg_keys[0], (VARS, NX, NZ, NY), 1.0, 6.0, ((1, 32), (2, 4)), jnp.float32)
    viscosity = jnp.clip(jnp.exp(math.log(0.12) - 1.7917595 * jax.random.uniform(arg_keys[1], (NX, NZ, NY), jnp.float32) ** steps_of(arg_keys[1], (NX, NZ, NY), ((0, 32), (1, 4)), -0.2, 0.2)), 0.02, 0.12)
    speeds = jnp.clip(jax.random.uniform(arg_keys[2], (VARS, 3), jnp.float32, -0.3, 0.3), -0.3, 0.3)
    energy_weights = jnp.clip(jnp.exp(jax.random.uniform(arg_keys[3], (VARS,), jnp.float32, math.log(0.5), math.log(2.0))), 0.5, 2.0)
    block_index = set_ends(jax.random.randint(arg_keys[4], (BLOCKS, BLOCK_LEN), 0, SNAPS), jax.random.fold_in(arg_keys[4], 1), 0, SNAPS - 1).astype(jnp.int32)
    block_offset = jax.random.randint(arg_keys[5], (BLOCKS,), 0, SNAPS).astype(jnp.int32)
    return {"initial_state": initial_state, "viscosity": viscosity, "speeds": speeds, "energy_weights": energy_weights, "block_index": block_index, "block_offset": block_offset}


def flux_update(padded, visc_pad, speeds):
    center = padded[:, 1:-1, 1:-1, :]
    visc_mid = visc_pad[1:-1, 1:-1, :]
    pairs = [(padded[:, 2:, 1:-1, :], padded[:, :-2, 1:-1, :], visc_pad[2:, 1:-1, :], visc_pad[:-2, 1:-1, :]), (padded[:, 1:-1, 2:, :], padded[:, 1:-1, :-2, :], visc_pad[1:-1, 2:, :], visc_pad[1:-1, :-2, :]), (jnp.roll(center, -1, axis=3), jnp.roll(center, 1, axis=3), jnp.roll(visc_mid, -1, axis=2), jnp.roll(visc_mid, 1, axis=2))]
    result = center
    for column, (forward, backward, visc_fwd, visc_back) in enumerate(pairs):
        rate = speeds[:, column].reshape(-1, 1, 1, 1)
        face_fwd = (visc_mid + visc_fwd) * 0.5
        face_back = (visc_mid + visc_back) * 0.5
        result = result - 0.5 * rate * (forward - backward) + face_fwd * (forward - center) - face_back * (center - backward)
    return result

def block_coefficients(block_index, block_offset, freqs_count, snap_count):
    frequency = jnp.arange(freqs_count).astype(jnp.int32)
    distance = (block_index - block_offset[:, None]).astype(jnp.int32)
    angles = (frequency[:, None, None] * distance[None]).astype(jnp.float32) * (math.pi / freqs_count)
    length = block_index.shape[1]
    window = jnp.sin(math.pi * (jnp.arange(length).astype(jnp.float32) + 0.5) / length) ** 2
    onehot = (block_index[:, :, None] == jnp.arange(snap_count).astype(jnp.int32)[None, None, :]).astype(jnp.float32)
    cosine_part = jnp.einsum('fbj,bjt->fbt', window * jnp.cos(angles), onehot, precision=lax.Precision.HIGHEST)
    sine_part = -jnp.einsum('fbj,bjt->fbt', window * jnp.sin(angles), onehot, precision=lax.Precision.HIGHEST)
    return jnp.stack([cosine_part, sine_part], axis=2)

def gram_terms(spec, energy_weights):
    shaped = spec.astype(jnp.float32).reshape(spec.shape[:4] + (-1,))
    real_zero, imag_zero = (shaped[:, 0, 0], shaped[:, 0, 1])
    real_one, imag_one = (shaped[:, 1, 0], shaped[:, 1, 1])
    high = lax.Precision.HIGHEST
    diag_zero = jnp.einsum('fvc,v->f', real_zero * real_zero + imag_zero * imag_zero, energy_weights, precision=high)
    diag_one = jnp.einsum('fvc,v->f', real_one * real_one + imag_one * imag_one, energy_weights, precision=high)
    cross_real = jnp.einsum('fvc,v->f', real_zero * real_one + imag_zero * imag_one, energy_weights, precision=high)
    cross_imag = jnp.einsum('fvc,v->f', real_zero * imag_one - imag_zero * real_one, energy_weights, precision=high)
    return jnp.stack([diag_zero, diag_one, cross_real, cross_imag], axis=1)

def leading(gram_sums):
    diag_zero, diag_one = (gram_sums[:, 0], gram_sums[:, 1])
    cross_real, cross_imag = (gram_sums[:, 2], gram_sums[:, 3])
    middle = (diag_zero + diag_one) * 0.5
    radius = jnp.sqrt(((diag_zero - diag_one) * 0.5) ** 2 + cross_real ** 2 + cross_imag ** 2)
    top_energy = middle + radius
    low_energy = middle - radius
    total_energy = diag_zero + diag_one + 1e-06
    kernel = ((diag_zero - low_energy) / total_energy, (diag_one - low_energy) / total_energy, cross_real / total_energy, cross_imag / total_energy)
    return (top_energy, kernel)

def widen(vector, ndim):
    return vector.reshape(vector.shape + (1,) * (ndim - 1))

def project(spec, kernel):
    shaped = spec.astype(jnp.float32)
    real_zero, imag_zero = (shaped[:, 0, 0], shaped[:, 0, 1])
    real_one, imag_one = (shaped[:, 1, 0], shaped[:, 1, 1])
    ndim = real_zero.ndim
    keep_zero, keep_one, cross_real, cross_imag = [widen(item, ndim) for item in kernel]
    zero_real = real_zero * keep_zero + real_one * cross_real + imag_one * cross_imag
    zero_imag = imag_zero * keep_zero + imag_one * cross_real - real_one * cross_imag
    one_real = real_zero * cross_real - imag_zero * cross_imag + real_one * keep_one
    one_imag = imag_zero * cross_real + real_zero * cross_imag + imag_one * keep_one
    block_zero = jnp.stack([zero_real, zero_imag], axis=1)
    block_one = jnp.stack([one_real, one_imag], axis=1)
    return jnp.stack([block_zero, block_one], axis=1).astype(jnp.bfloat16)

def reference(initial_state, viscosity, speeds, energy_weights, block_index, block_offset):
    visc_pad = jnp.pad(viscosity, ((1, 1), (1, 1), (0, 0)))
    fields = initial_state
    snapshots = []
    for number in range(SNAPS):
        padded = jnp.pad(fields, ((0, 0), (1, 1), (1, 1), (0, 0)))
        fields = flux_update(padded, visc_pad, speeds)
        snapshots.append(fields.astype(jnp.bfloat16))
    stacked = jnp.stack(snapshots).reshape(SNAPS, -1).astype(jnp.float32)
    coeffs = block_coefficients(block_index, block_offset, FREQS, SNAPS)
    cells_total = NX * NZ * NY

    def one_freq(coef_row):
        spec = jnp.dot(coef_row.reshape(-1, SNAPS), stacked, precision=lax.Precision.HIGHEST)
        spec = spec.reshape(1, BLOCKS, 2, VARS, NX, NZ, NY).astype(jnp.bfloat16)
        gram_sums = gram_terms(spec, energy_weights) / cells_total
        top_energy, kernel = leading(gram_sums)
        return (project(spec, kernel)[0], top_energy[0])
    modes, energy = lax.map(one_freq, coeffs)
    return (fields, modes, energy)
```

```python
import math

import jax
import jax.numpy as jnp
from jax import lax
from jax.experimental import pallas as pl
from jax.experimental.pallas import tpu as pltpu
from jax.sharding import Mesh
from jax.sharding import PartitionSpec as P

VARS = 5
FREQS = 64
BLOCKS = 2
SNAPS = 8
GRP_DEV = ("grp_0", "grp_1", "dev_0", "dev_1", "dev_2")
GRP = ("grp_0", "grp_1")
DEV = ("dev_0", "dev_1", "dev_2")
CELLS = 256 * 32 * 128

TILES = 32
QP = (TILES + 2) * 8
FP = (TILES + 1) * 8
CP = TILES * 8
PLANES = 24
PAIRS = [(a, b) for a in range(SNAPS) for b in range(a, SNAPS)]


def block_coefficients(block_index, block_offset):
    frequency = jnp.arange(FREQS)
    distance = block_index - block_offset[:, None]
    angles = (frequency[:, None, None] * distance[None]).astype(jnp.float32) * (math.pi / FREQS)
    length = block_index.shape[1]
    window = jnp.sin(math.pi * (jnp.arange(length).astype(jnp.float32) + 0.5) / length) ** 2
    onehot = (block_index[:, :, None] == jnp.arange(SNAPS)[None, None, :]).astype(jnp.float32)
    cosine = jnp.sum((window * jnp.cos(angles))[..., None] * onehot[None], axis=2)
    sine = -jnp.sum((window * jnp.sin(angles))[..., None] * onehot[None], axis=2)
    return jnp.stack([cosine, sine], axis=2)


def mode_matrix(coef, corr):
    def form(a, b):
        return jnp.sum(a[:, :, None] * corr[None] * b[:, None, :], axis=(1, 2))

    a0, b0, a1, b1 = coef[:, 0, 0], coef[:, 0, 1], coef[:, 1, 0], coef[:, 1, 1]
    g00 = form(a0, a0) + form(b0, b0)
    g11 = form(a1, a1) + form(b1, b1)
    gre = form(a0, a1) + form(b0, b1)
    gim = form(a0, b1) - form(b0, a1)
    middle = (g00 + g11) * 0.5
    radius = jnp.sqrt(((g00 - g11) * 0.5) ** 2 + gre**2 + gim**2)
    low = middle - radius
    total = g00 + g11 + 1e-06
    k0, k1 = ((g00 - low) / total)[:, None], ((g11 - low) / total)[:, None]
    cr, ci = (gre / total)[:, None], (gim / total)[:, None]
    rows = [
        a0 * k0 + a1 * cr + b1 * ci,
        b0 * k0 + b1 * cr - a1 * ci,
        a0 * cr - b0 * ci + a1 * k1,
        b0 * cr + a0 * ci + b1 * k1,
    ]
    return middle + radius, jnp.stack(rows, axis=1)


def rows_at(start, stride=None):
    return pl.ds(start, 8) if stride is None else pl.ds(start, 8, stride=stride)


def edge_masks():
    lane = lax.broadcasted_iota(jnp.int32, (8, 128), 0)
    return lane == 0, lane == 7


def ghosts(first, last):
    is_first, is_last = edge_masks()
    left = jnp.where(is_first, 0.0, pltpu.roll(last, 1, axis=0))
    right = jnp.where(is_last, 0.0, pltpu.roll(first, 7, axis=0))
    return left, right


def evolve_kernel(
    ints, speeds, weights, nu_own, nu_par, nu_third, q_own, q_par, q_ta, q_tb,
    snaps_ref, final_ref, corr_ref, q, q_odd, nx, ny, nym, nz, diag, snap, tmp,
):
    var = pl.program_id(0)
    par_base, third_base, inner = ints[64], ints[65], ints[66]
    own_tile, own_s, own_j = ints[67], ints[68], ints[69]

    def load_section(src, table, base):
        def unpack(slot, carry):
            d = ints[table + slot]
            tmp[pl.ds(pl.multiple_of(d * 64, 64), 64), :] = src[slot].astype(jnp.float32)
            return carry

        lax.fori_loop(0, 32, unpack, 0)

        def place(z, carry):
            row = pl.multiple_of((base + z) * QP, 8)
            first = last = None
            for j in range(TILES):
                val = tmp[rows_at(j * 8 + z, 256), :]
                q[rows_at(row + (j + 1) * 8), :] = val
                first = val if j == 0 else first
                last = val
            left, right = ghosts(first, last)
            q[rows_at(row), :] = left
            q[rows_at(row + (TILES + 1) * 8), :] = right
            return carry

        lax.fori_loop(0, 8, place, 0)

    def load_all(own, par, third):
        load_section(own, 0, 8)
        load_section(par, 32, par_base)

        @pl.when(inner == 1)
        def _():
            third()

    @pl.when(var == 0)
    def _():
        @pl.when(inner == 0)
        def _():
            def clear(k, carry):
                zero = jnp.zeros((QP, 128), jnp.float32)
                q[pl.ds(pl.multiple_of((third_base + k) * QP, 8), QP), :] = zero
                q_odd[pl.ds(pl.multiple_of((third_base + k) * QP, 8), QP), :] = zero
                return carry

            lax.fori_loop(0, 8, clear, 0)

        load_all(nu_own, nu_par, lambda: load_section(nu_third, 0, third_base))

        def faces(z, carry):
            row = pl.multiple_of(z * QP, 8)
            frow = pl.multiple_of(z * FP, 8)
            crow = pl.multiple_of(z * CP, 8)
            left = q[rows_at(row), :]
            mid = q[rows_at(row + 8), :]
            face_left = (left + mid) * 0.5
            nx[rows_at(frow), :] = face_left
            for j in range(TILES):
                right = q[rows_at(row + (j + 2) * 8), :]
                above = q[rows_at(row + QP + (j + 1) * 8), :]
                below = q[rows_at(row - QP + (j + 1) * 8), :]
                face_right = (mid + right) * 0.5
                face_up = (mid + above) * 0.5
                face_down = (mid + below) * 0.5
                face_y = (mid + pltpu.roll(mid, 127, axis=1)) * 0.5
                face_ym = pltpu.roll(face_y, 1, axis=1)
                nx[rows_at(frow + (j + 1) * 8), :] = face_right
                nz[rows_at(crow + CP + j * 8), :] = face_up
                nz[rows_at(crow + j * 8), :] = face_down
                ny[rows_at(crow + j * 8), :] = face_y
                nym[rows_at(crow + j * 8), :] = face_ym
                diag[rows_at(crow + j * 8), :] = 1.0 - (
                    (face_left + face_right) + (face_up + face_down) + (face_y + face_ym)
                )
                mid, face_left = right, face_right
            return carry

        lax.fori_loop(1, PLANES - 1, faces, 0)
        corr_ref[...] = jnp.zeros_like(corr_ref)

    def third():
        @pl.when(var < 2)
        def _():
            load_section(q_ta, 0, third_base)

        @pl.when(var >= 2)
        def _():
            load_section(q_tb, 32, third_base)

    load_all(q_own, q_par, third)

    hx, hz, hy = (0.5 * speeds[var * 3 + d] for d in range(3))

    def plane(z, src, dst, keep):
        row = pl.multiple_of(z * QP, 8)
        frow = pl.multiple_of(z * FP, 8)
        crow = pl.multiple_of(z * CP, 8)
        qm = src[rows_at(row), :]
        qc = src[rows_at(row + 8), :]
        fm = nx[rows_at(frow), :]
        first = last = None
        for j in range(TILES):
            qp = src[rows_at(row + (j + 2) * 8), :]
            fp = nx[rows_at(frow + (j + 1) * 8), :]
            up = src[rows_at(row + QP + (j + 1) * 8), :]
            down = src[rows_at(row - QP + (j + 1) * 8), :]
            new = (
                diag[rows_at(crow + j * 8), :] * qc
                + ((fp - hx) * qp + (fm + hx) * qm)
                + (
                    (nz[rows_at(crow + CP + j * 8), :] - hz) * up
                    + (nz[rows_at(crow + j * 8), :] + hz) * down
                )
                + (
                    (ny[rows_at(crow + j * 8), :] - hy) * pltpu.roll(qc, 127, axis=1)
                    + (nym[rows_at(crow + j * 8), :] + hy) * pltpu.roll(qc, 1, axis=1)
                )
            )
            dst[rows_at(row + (j + 1) * 8), :] = new
            if keep is not None:
                snap[rows_at(keep + j * 8), :] = new
            first = new if j == 0 else first
            last = new
            qm, qc, fm = qc, qp, fp
        left, right = ghosts(first, last)
        dst[rows_at(row), :] = left
        dst[rows_at(row + (TILES + 1) * 8), :] = right

    def step(t, src, dst):
        low, high = ints[72 + t], ints[84 + t]
        below = 8 - low

        def halo(k, inner_carry):
            plane(jnp.where(k < below, low + k, 16 + k - below), src, dst, None)
            return inner_carry

        lax.fori_loop(0, below + high - 16, halo, 0)

        def own(z, inner_carry):
            keep = pl.multiple_of((t - 1) * (8 * CP) + (z - 8) * CP, 8)
            plane(z, src, dst, keep)
            return inner_carry

        lax.fori_loop(8, 16, own, 0)

    def two_steps(k, carry):
        step(2 * k + 1, q, q_odd)
        step(2 * k + 2, q_odd, q)
        return carry

    lax.fori_loop(0, SNAPS // 2, two_steps, 0)

    for i in range(8):
        final_ref[i] = snap[rows_at(7 * 8 * CP + (own_j + i) * 8 + own_s, CP), :]

    weight = weights[var]
    sums = [jnp.zeros((8, 128), jnp.float32)] * len(PAIRS)
    for z in range(8):
        vals = [
            snap[rows_at(pl.multiple_of(t * 8 * CP + z * CP + own_tile * 8, 8)), :]
            .astype(jnp.bfloat16)
            .astype(jnp.float32)
            for t in range(SNAPS)
        ]
        for n, (a, b) in enumerate(PAIRS):
            sums[n] = sums[n] + vals[a] * vals[b]
    for n in range(len(PAIRS)):
        corr_ref[n] += weight * sums[n]

    def pack(t, carry):
        base = t * (8 * CP)
        for s in range(8):
            for j in range(0, TILES, 2):
                pair = [snap[rows_at(base + (j + e) * 8 + s, CP), :] for e in range(2)]
                x = s * TILES + j
                snaps_ref[t, x * 8 : x * 8 + 16, :] = jnp.concatenate(pair).astype(jnp.bfloat16)
        return carry

    lax.fori_loop(0, SNAPS, pack, 0)


def evolve(ints, speeds, weights, own, par):
    smem = pl.BlockSpec(memory_space=pltpu.SMEM)

    def stream(index):
        return pl.BlockSpec((32, None, 64, 128), lambda v: (0, index(v), 0, 0))

    return pl.pallas_call(
        evolve_kernel,
        name="evolve",
        grid=(VARS,),
        in_specs=[
            smem, smem, smem,
            stream(lambda v: 0), stream(lambda v: 0), stream(lambda v: 6),
            stream(lambda v: v + 1), stream(lambda v: v + 1),
            stream(lambda v: jnp.minimum(v + 7, 8)), stream(lambda v: jnp.maximum(v + 4, 6)),
        ],
        out_specs=[
            pl.BlockSpec((SNAPS, None, 2048, 128), lambda v: (0, v, 0, 0)),
            pl.BlockSpec((None, 8, 8, 128), lambda v: (v, 0, 0, 0)),
            pl.BlockSpec((len(PAIRS), 8, 128), lambda v: (0, 0, 0)),
        ],
        out_shape=[
            jax.ShapeDtypeStruct((SNAPS, VARS, 2048, 128), jnp.bfloat16),
            jax.ShapeDtypeStruct((VARS, 8, 8, 128), jnp.float32),
            jax.ShapeDtypeStruct((len(PAIRS), 8, 128), jnp.float32),
        ],
        scratch_shapes=[
            pltpu.VMEM((PLANES * QP, 128), jnp.float32),
            pltpu.VMEM((PLANES * QP, 128), jnp.float32),
            pltpu.VMEM((PLANES * FP, 128), jnp.float32),
            pltpu.VMEM((PLANES * CP, 128), jnp.float32),
            pltpu.VMEM((PLANES * CP, 128), jnp.float32),
            pltpu.VMEM(((PLANES + 1) * CP, 128), jnp.float32),
            pltpu.VMEM((PLANES * CP, 128), jnp.float32),
            pltpu.VMEM((SNAPS * 8 * CP, 128), jnp.float32),
            pltpu.VMEM((2048, 128), jnp.float32),
        ],
        compiler_params=pltpu.CompilerParams(vmem_limit_bytes=66_000_000),
    )(ints, speeds, weights, own, par, own, own, par, own, par)


def project_kernel(high_ref, low_ref, snaps_ref, out_ref):
    rows = snaps_ref.shape[1]

    def group(k, carry):
        at = pl.ds(pl.multiple_of(k * 32, 32), 32)
        data = snaps_ref[:, at, :].reshape(SNAPS * 32, 128)
        value = jnp.dot(high_ref[...], data, preferred_element_type=jnp.float32)
        value += jnp.dot(low_ref[...], data, preferred_element_type=jnp.float32)
        out_ref[:, at, :] = value.astype(jnp.bfloat16).reshape(8, 32, 128)
        return carry

    lax.fori_loop(0, rows // 32, group, 0, unroll=4)


def project(matrix, snaps):
    wide = jnp.kron(matrix, jnp.eye(32, dtype=jnp.float32))
    high = wide.astype(jnp.bfloat16)
    low = (wide - high.astype(jnp.float32)).astype(jnp.bfloat16)
    size = 1024
    whole = pl.BlockSpec((256, 256), lambda v, c: (0, 0))
    tile = pl.BlockSpec((SNAPS, None, size, 128), lambda v, c: (0, v, c, 0))
    return pl.pallas_call(
        project_kernel,
        name="project",
        grid=(VARS, 2048 // size),
        in_specs=[whole, whole, tile],
        out_specs=tile,
        out_shape=jax.ShapeDtypeStruct(snaps.shape, jnp.bfloat16),
    )(high, low, snaps)


def ring_gather(block, axis_of_core, direct):
    axes = ("grp_1", "dev_1", "dev_2")

    def shift(by):
        pairs = []
        for core in range(2):
            for y in range(4):
                for x in range(4):
                    to = ((y + by) % 4, x) if axis_of_core[core] == "y" else (y, (x + by) % 4)
                    pairs.append((core * 16 + y * 4 + x, core * 16 + to[0] * 4 + to[1]))
        return pairs

    before = lax.ppermute(block, axes, shift(1))
    after = lax.ppermute(block, axes, shift(-1))
    if direct:
        across = lax.ppermute(block, axes, shift(2))
    else:
        half = block.shape[0] // 2
        across = jnp.concatenate(
            [
                lax.ppermute(before[:half], axes, shift(1)),
                lax.ppermute(after[half:], axes, shift(-1)),
            ]
        )
    return jnp.stack([block, after, across, before])


def gather_sections(initial_state, viscosity):
    state = jnp.concatenate([viscosity[None], initial_state]).astype(jnp.bfloat16)
    state = state.reshape(VARS + 1, 64, 128)
    near = lax.ppermute(state[:3], GRP, [(2, 1), (1, 2)])
    far = lax.ppermute(state[3:], GRP, [(2, 0), (1, 3)])
    block = jnp.concatenate([state, near + far])
    other = lax.ppermute(block, "dev_0", [(0, 1), (1, 0)])
    pair = jnp.stack([block, other])
    first = ring_gather(pair, ("y", "x"), True)
    own = ring_gather(first, ("x", "y"), False).reshape(32, 9, 64, 128)
    par = lax.ppermute(own, "grp_1", [(0, 1), (1, 0)])
    return own, par


def layout_ints():
    h, c, l, y, x = (lax.axis_index(axis) for axis in GRP_DEV)
    slots = jnp.arange(32)
    outer_rel, inner_rel, l_rel = slots // 8, slots // 2 % 4, slots % 2

    def owners(core):
        along_y = jnp.where(core == 0, inner_rel, outer_rel)
        along_x = jnp.where(core == 0, outer_rel, inner_rel)
        return ((l + l_rel) % 2) * 16 + ((y + along_y) % 4) * 4 + (x + along_x) % 4

    d = l * 16 + y * 4 + x
    inner = (h != c).astype(jnp.int32)
    par_base = jnp.where(c == 1, 0, 16)
    third_base = 16 - par_base
    steps = jnp.arange(12)
    low = jnp.where((inner == 0) & (c == 0), 8, steps)
    high = jnp.where((inner == 0) & (c == 1), 16, 24 - steps)
    scalars = jnp.stack([par_base, third_base, inner, d, d // 4, (d % 4) * 8, d, d])
    return jnp.concatenate([owners(c), owners(1 - c), scalars, low, high]).astype(jnp.int32)


def body(initial_state, viscosity, speeds, energy_weights, block_index, block_offset):
    own, par = gather_sections(initial_state, viscosity)
    snaps, final, corr = evolve(layout_ints(), speeds.reshape(-1), energy_weights, own, par)
    sums = jnp.sum(corr, axis=(1, 2))
    for axis in GRP_DEV:
        sums = lax.psum(sums, axis)
    sums = sums / CELLS
    order = [[PAIRS.index((min(a, b), max(a, b))) for b in range(SNAPS)] for a in range(SNAPS)]
    corr_matrix = sums[jnp.array(order)]
    coef = block_coefficients(block_index, block_offset)
    own_coef = lax.dynamic_slice_in_dim(coef, lax.axis_index(DEV) * 2, 2, 0)
    energy, matrix = mode_matrix(own_coef, corr_matrix)
    modes = project(matrix.reshape(8, SNAPS), snaps)
    return final, modes.reshape(2, BLOCKS, 2, VARS, 256, 8, 128), energy


def solution(mesh):
    torus = Mesh(mesh.devices.reshape(2, 2, 2, 4, 4), GRP_DEV)
    in_specs = (P(None, DEV, GRP, None), P(DEV, GRP, None), P(), P(), P(), P())
    out_specs = (P(None, DEV, GRP, None), P(DEV, None, None, None, None, GRP, None), P(DEV))
    return jax.shard_map(body, mesh=torus, in_specs=in_specs, out_specs=out_specs, check_vma=False)
```

```python
import math

import jax
import jax.numpy as jnp
from jax import lax
from jax.experimental import pallas as pl
from jax.experimental.pallas import tpu as pltpu
from jax.sharding import Mesh
from jax.sharding import PartitionSpec as P

VARS = 5
FREQS = 64
BLOCKS = 2
SNAPS = 8
GRP_DEV = ("grp_0", "grp_1", "dev_0", "dev_1", "dev_2")
GRP = ("grp_0", "grp_1")
DEV = ("dev_0", "dev_1", "dev_2")
CELLS = 256 * 32 * 128

TILES = 16
PLANES = 26
LOW, OWN, HIGH = 1, 9, 17
PAIRS = [(a, b) for a in range(SNAPS) for b in range(a, SNAPS)]
BF = jnp.bfloat16


def block_coefficients(block_index, block_offset):
    frequency = jnp.arange(FREQS)
    distance = block_index - block_offset[:, None]
    angles = (frequency[:, None, None] * distance[None]).astype(jnp.float32) * (math.pi / FREQS)
    length = block_index.shape[1]
    window = jnp.sin(math.pi * (jnp.arange(length).astype(jnp.float32) + 0.5) / length) ** 2
    onehot = (block_index[:, :, None] == jnp.arange(SNAPS)[None, None, :]).astype(jnp.float32)
    cosine = jnp.sum((window * jnp.cos(angles))[..., None] * onehot[None], axis=2)
    sine = -jnp.sum((window * jnp.sin(angles))[..., None] * onehot[None], axis=2)
    return jnp.stack([cosine, sine], axis=2)


def mode_matrix(coef, corr):
    def form(a, b):
        return jnp.sum(a[:, :, None] * corr[None] * b[:, None, :], axis=(1, 2))

    a0, b0, a1, b1 = coef[:, 0, 0], coef[:, 0, 1], coef[:, 1, 0], coef[:, 1, 1]
    g00 = form(a0, a0) + form(b0, b0)
    g11 = form(a1, a1) + form(b1, b1)
    gre = form(a0, a1) + form(b0, b1)
    gim = form(a0, b1) - form(b0, a1)
    middle = (g00 + g11) * 0.5
    radius = jnp.sqrt(((g00 - g11) * 0.5) ** 2 + gre**2 + gim**2)
    low = middle - radius
    total = g00 + g11 + 1e-06
    k0, k1 = ((g00 - low) / total)[:, None], ((g11 - low) / total)[:, None]
    cr, ci = (gre / total)[:, None], (gim / total)[:, None]
    rows = [
        a0 * k0 + a1 * cr + b1 * ci,
        b0 * k0 + b1 * cr - a1 * ci,
        a0 * cr - b0 * ci + a1 * k1,
        b0 * cr + a0 * ci + b1 * k1,
    ]
    return middle + radius, jnp.stack(rows, axis=1)


def by_half(fn, *values):
    parts = [fn(*[v[:, half * 128 : half * 128 + 128] for v in values]) for half in range(2)]
    return jnp.concatenate(parts, axis=1)


def ghosts(first, last):
    place = lax.broadcasted_iota(jnp.int32, (8, 128), 0)
    low, high = (pltpu.roll(last[:, k : k + 128], 1, axis=0) for k in (0, 128))
    left = jnp.concatenate(
        [jnp.where(place == 0, 0.0, low), jnp.where(place == 0, low, high)], axis=1
    )
    low, high = (pltpu.roll(first[:, k : k + 128], 7, axis=0) for k in (0, 128))
    right = jnp.concatenate(
        [jnp.where(place == 7, high, low), jnp.where(place == 7, 0.0, high)], axis=1
    )
    return left.astype(BF), right.astype(BF)


def y_next(value):
    return by_half(lambda part: pltpu.roll(part, 127, axis=1), value)


def y_last(value):
    return by_half(lambda part: pltpu.roll(part, 1, axis=1), value)


def evolve_kernel(
    ints, speeds, matrix_ref, nu_own, nu_par, nu_third, q_own, q_par, q_ta, q_tb,
    out_ref, wide, snaps_ref, full, full_odd, even, odd, nx, ny, nym, nz, axp, axm, ayp, aym, azp, azm,
):
    var = pl.program_id(0)
    par_base, third_base, inner = ints[64], ints[65], ints[66]

    def load_section(src, table, base):
        for dl in range(2):
            def pair(ip, carry):
                rows = pl.ds(pl.multiple_of(ip * 16, 16), 16)
                halves = []
                for half in range(2):
                    blocks = [
                        src[ints[table + (half * 8 + s) * 2 + dl], rows, :].astype(jnp.float32)
                        for s in range(8)
                    ]
                    grid = jnp.stack(blocks).reshape(8, 2, 8, 128)
                    halves.append([jnp.swapaxes(grid[:, i], 0, 1) for i in range(2)])
                for i in range(2):
                    slot = dl * 8 + ip * 2 + i
                    for z in range(8):
                        val = jnp.concatenate([halves[0][i][z], halves[1][i][z]], axis=1)
                        full[base + z, slot] = val
                        even[base + z, slot + 1] = val.astype(BF)
                return carry

            lax.fori_loop(0, 4, pair, 0)

        def edge(z, carry):
            left, right = ghosts(full[base + z, 0], full[base + z, TILES - 1])
            even[base + z, 0] = left
            even[base + z, TILES + 1] = right
            return carry

        lax.fori_loop(0, 8, edge, 0)

    def load_all(own, par, third):
        load_section(own, 0, OWN)
        load_section(par, 32, par_base)

        @pl.when(inner == 1)
        def _():
            third()

    @pl.when(var == 0)
    def _():
        @pl.when(inner == 0)
        def _():
            def clear(k, carry):
                even[third_base + k] = jnp.zeros((TILES + 2, 8, 256), BF)
                odd[third_base + k] = jnp.zeros((TILES + 2, 8, 256), BF)
                full[third_base + k] = jnp.zeros((TILES, 8, 256), jnp.float32)
                return carry

            lax.fori_loop(0, 8, clear, 0)

        load_all(nu_own, nu_par, lambda: load_section(nu_third, 0, third_base))

        def faces(z, carry):
            def nu(plane, slot):
                return even[plane, slot].astype(jnp.float32)

            mid = full[z, 0]
            nx[z, 0] = ((nu(z, 0) + mid) * 0.5).astype(BF)
            for j in range(TILES):
                right = nu(z, j + 2)
                face_y = (mid + y_next(mid)) * 0.5
                nx[z, j + 1] = ((mid + right) * 0.5).astype(BF)
                nz[z + 1, j] = ((mid + full[z + 1, j]) * 0.5).astype(BF)
                nz[z, j] = ((mid + full[z - 1, j]) * 0.5).astype(BF)
                ny[z, j] = face_y.astype(BF)
                nym[z, j] = y_last(face_y).astype(BF)
                mid = right
            return carry

        lax.fori_loop(2, PLANES - 2, faces, 0)

    def third():
        @pl.when(var < 2)
        def _():
            load_section(q_ta, 0, third_base)

        @pl.when(var >= 2)
        def _():
            load_section(q_tb, 32, third_base)

    load_all(q_own, q_par, third)

    hx, hz, hy = ((0.5 * speeds[var * 3 + d]).astype(BF) for d in range(3))

    def coefs(z, carry):
        for j in range(TILES):
            axp[z, j] = nx[z, j + 1] - hx
            axm[z, j] = nx[z, j] + hx
            azp[z, j] = nz[z + 1, j] - hz
            azm[z, j] = nz[z, j] + hz
            ayp[z, j] = ny[z, j] - hy
            aym[z, j] = nym[z, j] + hy
        return carry

    lax.fori_loop(2, PLANES - 2, coefs, 0)

    def planes(groups, src, dst, old_ref, new_ref, keep):
        state = []
        for z, count in groups:
            mid = [src[z + k, 1] for k in range(count)]
            state.append((mid, [mid[k] - src[z + k, 0] for k in range(count)]))
        first, last = {}, {}
        for j in range(TILES):
            for g, (z, count) in enumerate(groups):
                mid, before = state[g]
                right = [src[z + k, j + 2] for k in range(count)]
                after = [right[k] - mid[k] for k in range(count)]
                column = [src[z - 1, j + 1]] + mid + [src[z + count, j + 1]]
                steps = [column[k + 1] - column[k] for k in range(count + 1)]
                for k in range(count):
                    at = z + k
                    old = old_ref[at, j]
                    change_x = axp[at, j] * after[k] - axm[at, j] * before[k]
                    change_z = azp[at, j] * steps[k + 1] - azm[at, j] * steps[k]
                    change_y = ayp[at, j] * (y_next(old) - old).astype(BF) + aym[at, j] * (
                        y_last(old) - old
                    ).astype(BF)
                    change = (change_x + change_z) + change_y
                    new = old + change.astype(jnp.float32)
                    new_ref[at, j] = new
                    short = new.astype(BF)
                    dst[at, j + 1] = short
                    if keep is not None:
                        snaps_ref[keep[0], keep[1] + k, j] = short
                    if j == 0:
                        first[g, k] = new
                    last[g, k] = new
                state[g] = (right, after)
        for g, (z, count) in enumerate(groups):
            for k in range(count):
                left, right = ghosts(first[g, k], last[g, k])
                dst[z + k, 0] = left
                dst[z + k, TILES + 1] = right

    def step(t, src, dst, old_ref, new_ref):
        pairs = (9 - t) // 2

        @pl.when(inner == 1)
        def _():
            def both(k, carry):
                planes(
                    [(OWN - 2 - 2 * k, 2), (HIGH + 2 * k, 2)], src, dst, old_ref, new_ref, None
                )
                return carry

            lax.fori_loop(0, pairs, both, 0)

        @pl.when(inner == 0)
        def _():
            def one(k, carry):
                base = jnp.where(par_base == LOW, OWN - 2 - 2 * k, HIGH + 2 * k)
                planes([(base, 2)], src, dst, old_ref, new_ref, None)
                return carry

            lax.fori_loop(0, pairs, one, 0)

        def own(k, carry):
            planes([(OWN + 4 * k, 4)], src, dst, old_ref, new_ref, (t - 1, 4 * k))
            return carry

        lax.fori_loop(0, 2, own, 0)

    def two_steps(k, carry):
        step(2 * k + 1, even, odd, full, full_odd)
        step(2 * k + 2, odd, even, full_odd, full)
        return carry

    lax.fori_loop(0, SNAPS // 2, two_steps, 0)

    def project(jp, carry):
        for e in range(2):
            for part in range(2):
                data = snaps_ref[:, 4 * part : 4 * part + 4, jp * 2 + e]
                value = jnp.dot(
                    matrix_ref[...], data.reshape(256, 256), preferred_element_type=jnp.float32
                )
                wide[e, :, 4 * part : 4 * part + 4] = value.reshape(8, 4, 8, 256)
        rows = pl.ds(pl.multiple_of(jp * 16, 16), 16)
        for o in range(8):
            for half in range(2):
                parts = [
                    jnp.swapaxes(wide[e, o, :, :, half * 128 : half * 128 + 128], 0, 1)
                    for e in range(2)
                ]
                out_ref[o, half * 8 : half * 8 + 8, rows, :] = (
                    jnp.concatenate(parts, axis=1).astype(BF)
                )
        return carry

    lax.fori_loop(0, TILES // 2, project, 0)


def evolve(ints, speeds, matrix, own, par):
    smem = pl.BlockSpec(memory_space=pltpu.SMEM)

    def stream(index):
        return pl.BlockSpec((32, None, 64, 128), lambda v: (0, index(v), 0, 0))

    def coef_array(planes=PLANES, tiles=TILES):
        return pltpu.VMEM((planes, tiles, 8, 256), BF)

    wide = jnp.kron(matrix, jnp.eye(32, dtype=jnp.float32)).astype(BF)
    return pl.pallas_call(
        evolve_kernel,
        name="evolve",
        grid=(VARS,),
        in_specs=[
            smem, smem, pl.BlockSpec((256, 256), lambda v: (0, 0)),
            stream(lambda v: 0), stream(lambda v: 0), stream(lambda v: 6),
            stream(lambda v: v + 1), stream(lambda v: v + 1),
            stream(lambda v: jnp.minimum(v + 7, 8)), stream(lambda v: jnp.maximum(v + 4, 6)),
        ],
        out_specs=pl.BlockSpec((8, None, 16, 128, 128), lambda v: (0, v, 0, 0, 0)),
        out_shape=jax.ShapeDtypeStruct((8, VARS, 16, 128, 128), BF),
        scratch_shapes=[
            pltpu.VMEM((2, 8, 8, 8, 256), jnp.float32),
            pltpu.VMEM((SNAPS, 8, TILES, 8, 256), BF),
            pltpu.VMEM((PLANES, TILES, 8, 256), jnp.float32),
            pltpu.VMEM((PLANES, TILES, 8, 256), jnp.float32),
            coef_array(tiles=TILES + 2), coef_array(tiles=TILES + 2), coef_array(tiles=TILES + 1),
            coef_array(), coef_array(), coef_array(PLANES + 1),
            coef_array(), coef_array(), coef_array(),
            coef_array(), coef_array(), coef_array(),
        ],
        compiler_params=pltpu.CompilerParams(vmem_limit_bytes=66_000_000),
        cost_estimate=pl.CostEstimate(
            flops=400_000_000_000, bytes_accessed=40_000_000, transcendentals=0
        ),
    )(ints, speeds, wide, own, par, own, own, par, own, par)


def ring_shift(axis_of_core, by):
    pairs = []
    for core in range(2):
        for y in range(4):
            for x in range(4):
                to = ((y + by) % 4, x) if axis_of_core[core] == "y" else (y, (x + by) % 4)
                pairs.append((core * 16 + y * 4 + x, core * 16 + to[0] * 4 + to[1]))
    return lambda value: lax.ppermute(value, ("grp_1", "dev_1", "dev_2"), pairs)


def swap_cores(value):
    return lax.ppermute(value, "grp_1", [(0, 1), (1, 0)])


SIDE = 24


def local_kernel(
    ints, speeds, weights, fields, final_ref, corr_ref,
    qa, qb, nx, nzp, nzm, nyp, nym, diag, snap,
):
    low, high = ints[0], ints[1]
    row = lax.broadcasted_iota(jnp.int32, (SIDE, 128), 0)
    mask = ((row >= ints[2]) & (row < ints[3])).astype(jnp.float32)
    rates = [[0.5 * speeds[v * 3 + d] for d in range(3)] for v in range(VARS)]

    def up(value):
        return pltpu.roll(value, SIDE - 1, axis=0)

    def down(value):
        return pltpu.roll(value, 1, axis=0)

    def faces(x, carry):
        mid = fields[0, x]
        right = (mid + fields[0, x + 1]) * 0.5
        left = (mid + fields[0, x - 1]) * 0.5
        above = (mid + up(mid)) * 0.5
        below = (mid + down(mid)) * 0.5
        ahead = (mid + pltpu.roll(mid, 127, axis=1)) * 0.5
        behind = (mid + pltpu.roll(mid, 1, axis=1)) * 0.5
        nx[x + 1] = right
        nx[x] = left
        nzp[x], nzm[x], nyp[x], nym[x] = above, below, ahead, behind
        diag[x] = 1.0 - ((right + left) + (above + below) + (ahead + behind))
        return carry

    lax.fori_loop(1, SIDE - 1, faces, 0)
    for v in range(VARS):
        qa[v] = fields[v + 1]
        qb[v] = fields[v + 1]

    def step(t, src, dst):
        def one(x, carry):
            for v in range(VARS):
                hx, hz, hy = rates[v]
                mid = src[v, x]
                new = (
                    diag[x] * mid
                    + ((nx[x + 1] - hx) * src[v, x + 1] + (nx[x] + hx) * src[v, x - 1])
                    + ((nzp[x] - hz) * up(mid) + (nzm[x] + hz) * down(mid))
                    + (
                        (nyp[x] - hy) * pltpu.roll(mid, 127, axis=1)
                        + (nym[x] + hy) * pltpu.roll(mid, 1, axis=1)
                    )
                )
                dst[v, x] = new * mask
            return carry

        lax.fori_loop(jnp.maximum(t, low), jnp.minimum(SIDE - t, high), one, 0)
        for v in range(VARS):
            for x in range(8):
                snap[t - 1, v, x] = dst[v, 8 + x, 8:16, :].astype(BF).astype(jnp.float32)

    def two_steps(k, carry):
        step(2 * k + 1, qa, qb)
        step(2 * k + 2, qb, qa)
        return carry

    lax.fori_loop(0, SNAPS // 2, two_steps, 0)
    for v in range(VARS):
        for x in range(8):
            final_ref[v, x] = qa[v, 8 + x, 8:16, :]

    corr_ref[...] = jnp.zeros_like(corr_ref)

    def correlate(v, carry):
        weight = weights[v]
        sums = [jnp.zeros((8, 128), jnp.float32)] * len(PAIRS)
        for x in range(8):
            vals = [snap[t, v, x] for t in range(SNAPS)]
            for n, (a, b) in enumerate(PAIRS):
                sums[n] = sums[n] + vals[a] * vals[b]
        for n in range(len(PAIRS)):
            corr_ref[n] += weight * sums[n]
        return carry

    lax.fori_loop(0, VARS, correlate, 0)


def local_steps(ints, speeds, weights, fields):
    smem = pl.BlockSpec(memory_space=pltpu.SMEM)
    vmem = pl.BlockSpec(memory_space=pltpu.VMEM)
    cube = pltpu.VMEM((SIDE, SIDE, 128), jnp.float32)
    cubes = pltpu.VMEM((VARS, SIDE, SIDE, 128), jnp.float32)
    return pl.pallas_call(
        local_kernel,
        name="local",
        in_specs=[smem, smem, smem, vmem],
        out_specs=[vmem, vmem],
        out_shape=[
            jax.ShapeDtypeStruct((VARS, 8, 8, 128), jnp.float32),
            jax.ShapeDtypeStruct((len(PAIRS), 8, 128), jnp.float32),
        ],
        scratch_shapes=[
            cubes, cubes, pltpu.VMEM((SIDE + 1, SIDE, 128), jnp.float32),
            cube, cube, cube, cube, cube,
            pltpu.VMEM((SNAPS, VARS, 8, 8, 128), jnp.float32),
        ],
        compiler_params=pltpu.CompilerParams(vmem_limit_bytes=24_000_000),
        cost_estimate=pl.CostEstimate(
            flops=4_000_000_000, bytes_accessed=6_000_000, transcendentals=0
        ),
    )(ints, speeds, weights, fields)


def local_ints():
    own = lax.axis_index(DEV)
    grp = lax.axis_index(GRP)
    bounds = [
        jnp.where(own == 0, 8, 0),
        jnp.where(own == 31, 16, SIDE),
        jnp.where(grp == 0, 8, 0),
        jnp.where(grp == 3, 16, SIDE),
    ]
    return jnp.stack(bounds).astype(jnp.int32)


def ring_sum(value, axes):
    one, two, three = (
        lax.ppermute(value, axes, [(i, (i + by) % 4) for i in range(4)]) for by in (1, 2, 3)
    )
    return (value + two) + (one + three)


def communicate(initial_state, viscosity, speeds, energy_weights):
    fields = jnp.concatenate([viscosity[None], initial_state])
    state = fields.astype(BF).reshape(VARS + 1, 64, 128)
    near = lax.ppermute(state[:3], GRP, [(2, 1), (1, 2)])
    far = lax.ppermute(state[3:], GRP, [(2, 0), (1, 3)])
    third = lax.ppermute(fields, GRP, [(1, 2), (2, 1)])
    par = swap_cores(fields)
    block = jnp.concatenate([state, near + far])
    other = lax.ppermute(block, "dev_0", [(0, 1), (1, 0)])

    odd = lax.axis_index("grp_1") == 1
    column = jnp.concatenate(
        [jnp.where(odd, par, third), fields, jnp.where(odd, third, par)], axis=2
    )
    up = [(i, i + 1) for i in range(31)]
    before_x = lax.ppermute(column, DEV, up)
    after_x = lax.ppermute(column, DEV, [(b, a) for a, b in up])
    cube = jnp.concatenate([before_x, column, after_x], axis=1)

    pair = jnp.stack([block, other])
    near_axis = [ring_shift(("y", "x"), by) for by in (-1, 2, 1)]
    first = jnp.stack([pair] + [shift(pair) for shift in near_axis])
    first, cube = lax.optimization_barrier((first, cube))
    forward, back = ring_shift(("x", "y"), 1), ring_shift(("x", "y"), -1)
    before, after = forward(first), back(first)
    final, corr = local_steps(local_ints(), speeds, energy_weights, cube)
    sums = jnp.sum(corr, axis=(1, 2)) / CELLS
    before, after, sums = lax.optimization_barrier((before, after, sums))
    half_before, half_after = forward(before[:2]), back(after[2:])
    sums = ring_sum(ring_sum(sums, "dev_2"), "dev_1")
    half_before, half_after, sums = lax.optimization_barrier((half_before, half_after, sums))
    across = jnp.concatenate([half_before, half_after])
    own = jnp.stack([first, after, across, before]).reshape(32, 9, 64, 128)
    partner = swap_cores(own)
    sums = ring_sum(sums, ("grp_0", "dev_0"))
    sums = sums + swap_cores(sums)
    return own, partner, final, sums


def layout_ints():
    h, c, l, y, x = (lax.axis_index(axis) for axis in GRP_DEV)
    d = jnp.arange(32)
    to_l, to_y, to_x = (d // 16 + l) % 2, (d // 4 - y) % 4, (d - x) % 4

    def slots(core):
        outer = jnp.where(core == 0, to_x, to_y)
        return outer * 8 + jnp.where(core == 0, to_y, to_x) * 2 + to_l

    inner = (h != c).astype(jnp.int32)
    par_base = jnp.where(c == 1, LOW, HIGH)
    scalars = [par_base, LOW + HIGH - par_base, inner]
    return jnp.concatenate([slots(c), slots(1 - c), jnp.stack(scalars)]).astype(jnp.int32)


def body(initial_state, viscosity, speeds, energy_weights, block_index, block_offset):
    speeds = speeds.reshape(-1)
    own, par, final, sums = communicate(initial_state, viscosity, speeds, energy_weights)
    order = [[PAIRS.index((min(a, b), max(a, b))) for b in range(SNAPS)] for a in range(SNAPS)]
    corr_matrix = sums[jnp.array(order)]
    coef = block_coefficients(block_index, block_offset)
    own_coef = lax.dynamic_slice_in_dim(coef, lax.axis_index(DEV) * 2, 2, 0)
    energy, matrix = mode_matrix(own_coef, corr_matrix)
    modes = evolve(layout_ints(), speeds, matrix.reshape(8, SNAPS), own, par)
    return final, modes.reshape(2, BLOCKS, 2, VARS, 256, 8, 128), energy


def solution(mesh):
    torus = Mesh(mesh.devices.reshape(2, 2, 2, 4, 4), GRP_DEV)
    in_specs = (P(None, DEV, GRP, None), P(DEV, GRP, None), P(), P(), P(), P())
    out_specs = (P(None, DEV, GRP, None), P(DEV, None, None, None, None, GRP, None), P(DEV))
    return jax.shard_map(body, mesh=torus, in_specs=in_specs, out_specs=out_specs, check_vma=False)
```

```python
import math

import jax
import jax.numpy as jnp
import numpy as np
from jax import lax
from jax.experimental import pallas as pl
from jax.experimental.pallas import tpu as pltpu
from jax.sharding import Mesh
from jax.sharding import PartitionSpec as P

VARS = 5
FREQS = 64
BLOCKS = 2
SNAPS = 8
GRP_DEV = ("grp_0", "grp_1", "dev_0", "dev_1", "dev_2")
GRP = ("grp_0", "grp_1")
DEV = ("dev_0", "dev_1", "dev_2")
CELLS = 256 * 32 * 128

TILES = 16
PLANES = 26
LOW, OWN, HIGH = 1, 9, 17
OWN_STEP = 8
PAIRS = [(a, b) for a in range(SNAPS) for b in range(a, SNAPS)]
BF = jnp.bfloat16


def block_coefficients(block_index, block_offset):
    frequency = jnp.arange(FREQS)
    distance = block_index - block_offset[:, None]
    angles = (frequency[:, None, None] * distance[None]).astype(jnp.float32) * (math.pi / FREQS)
    length = block_index.shape[1]
    window = jnp.sin(math.pi * (jnp.arange(length).astype(jnp.float32) + 0.5) / length) ** 2
    onehot = (block_index[:, :, None] == jnp.arange(SNAPS)[None, None, :]).astype(jnp.float32)
    cosine = jnp.sum((window * jnp.cos(angles))[..., None] * onehot[None], axis=2)
    sine = -jnp.sum((window * jnp.sin(angles))[..., None] * onehot[None], axis=2)
    return jnp.stack([cosine, sine], axis=2)


def mode_matrix(coef, corr):
    def form(a, b):
        return jnp.sum(a[:, :, None] * corr[None] * b[:, None, :], axis=(1, 2))

    a0, b0, a1, b1 = coef[:, 0, 0], coef[:, 0, 1], coef[:, 1, 0], coef[:, 1, 1]
    g00 = form(a0, a0) + form(b0, b0)
    g11 = form(a1, a1) + form(b1, b1)
    gre = form(a0, a1) + form(b0, b1)
    gim = form(a0, b1) - form(b0, a1)
    middle = (g00 + g11) * 0.5
    radius = jnp.sqrt(((g00 - g11) * 0.5) ** 2 + gre**2 + gim**2)
    low = middle - radius
    total = g00 + g11 + 1e-06
    k0, k1 = ((g00 - low) / total)[:, None], ((g11 - low) / total)[:, None]
    cr, ci = (gre / total)[:, None], (gim / total)[:, None]
    rows = [
        a0 * k0 + a1 * cr + b1 * ci,
        b0 * k0 + b1 * cr - a1 * ci,
        a0 * cr - b0 * ci + a1 * k1,
        b0 * cr + a0 * ci + b1 * k1,
    ]
    return middle + radius, jnp.stack(rows, axis=1)


def by_half(fn, *values):
    parts = [fn(*[v[:, half * 128 : half * 128 + 128] for v in values]) for half in range(2)]
    return jnp.concatenate(parts, axis=1)


def ghosts(first, last):
    place = lax.broadcasted_iota(jnp.int32, (8, 128), 0)
    low, high = (pltpu.roll(last[:, k : k + 128], 1, axis=0) for k in (0, 128))
    left = jnp.concatenate(
        [jnp.where(place == 0, 0.0, low), jnp.where(place == 0, low, high)], axis=1
    )
    low, high = (pltpu.roll(first[:, k : k + 128], 7, axis=0) for k in (0, 128))
    right = jnp.concatenate(
        [jnp.where(place == 7, high, low), jnp.where(place == 7, 0.0, high)], axis=1
    )
    return left.astype(BF), right.astype(BF)


def y_next(value):
    return by_half(lambda part: pltpu.roll(part, 127, axis=1), value)


def y_last(value):
    return by_half(lambda part: pltpu.roll(part, 1, axis=1), value)


def evolve_kernel(
    ints, speeds, matrix_ref, shift_ref, nu_own, nu_par, nu_third, q_own, q_par, q_ta, q_tb,
    out_ref, wide, slopes, snaps_ref, full, full_odd, even, odd, nx, ny, nym, nz, axp, axm, ayp, aym, azp, azm,
):
    var = pl.program_id(0)
    par_base, third_base, inner = ints[64], ints[65], ints[66]

    def load_section(src, table, base):
        for dl in range(2):
            def pair(ip, carry):
                rows = pl.ds(pl.multiple_of(ip * 16, 16), 16)
                halves = []
                for half in range(2):
                    blocks = [
                        src[ints[table + (half * 8 + s) * 2 + dl], rows, :].astype(jnp.float32)
                        for s in range(8)
                    ]
                    grid = jnp.stack(blocks).reshape(8, 2, 8, 128)
                    halves.append([jnp.swapaxes(grid[:, i], 0, 1) for i in range(2)])
                for i in range(2):
                    slot = dl * 8 + ip * 2 + i
                    for z in range(8):
                        val = jnp.concatenate([halves[0][i][z], halves[1][i][z]], axis=1)
                        full[base + z, slot] = val
                        even[base + z, slot + 1] = val.astype(BF)
                return carry

            lax.fori_loop(0, 4, pair, 0)

        def edge(z, carry):
            left, right = ghosts(full[base + z, 0], full[base + z, TILES - 1])
            even[base + z, 0] = left
            even[base + z, TILES + 1] = right
            return carry

        lax.fori_loop(0, 8, edge, 0)

    def load_all(own, par, third):
        load_section(own, 0, OWN)
        load_section(par, 32, par_base)

        @pl.when(inner == 1)
        def _():
            third()

    @pl.when(var == 0)
    def _():
        @pl.when(inner == 0)
        def _():
            def clear(k, carry):
                even[third_base + k] = jnp.zeros((TILES + 2, 8, 256), BF)
                odd[third_base + k] = jnp.zeros((TILES + 2, 8, 256), BF)
                full[third_base + k] = jnp.zeros((TILES, 8, 256), jnp.float32)
                return carry

            lax.fori_loop(0, 8, clear, 0)

        load_all(nu_own, nu_par, lambda: load_section(nu_third, 0, third_base))

        def faces(z, carry):
            def nu(plane, slot):
                return even[plane, slot].astype(jnp.float32)

            mid = full[z, 0]
            nx[z, 0] = ((nu(z, 0) + mid) * 0.5).astype(BF)
            for j in range(TILES):
                right = nu(z, j + 2)
                face_y = (mid + y_next(mid)) * 0.5
                nx[z, j + 1] = ((mid + right) * 0.5).astype(BF)
                nz[z + 1, j] = ((mid + full[z + 1, j]) * 0.5).astype(BF)
                nz[z, j] = ((mid + full[z - 1, j]) * 0.5).astype(BF)
                ny[z, j] = face_y.astype(BF)
                nym[z, j] = y_last(face_y).astype(BF)
                mid = right
            return carry

        lax.fori_loop(2, PLANES - 2, faces, 0)

    def third():
        @pl.when(var < 2)
        def _():
            load_section(q_ta, 0, third_base)

        @pl.when(var >= 2)
        def _():
            load_section(q_tb, 32, third_base)

    load_all(q_own, q_par, third)

    hx, hz, hy = ((0.5 * speeds[var * 3 + d]).astype(BF) for d in range(3))

    def coefs(z, carry):
        for j in range(TILES):
            axp[z, j] = nx[z, j + 1] - hx
            axm[z, j] = nx[z, j] + hx
            azp[z, j] = nz[z + 1, j] - hz
            azm[z, j] = nz[z, j] + hz
            ayp[z, j] = ny[z, j] - hy
            aym[z, j] = nym[z, j] + hy
        return carry

    lax.fori_loop(2, PLANES - 2, coefs, 0)

    def planes(groups, src, dst, old_ref, new_ref, keep):
        state = []
        total = sum(count for _, count in groups)
        cells = [
            src[z : z + count, 1 : TILES + 1] if isinstance(z, int)
            else src[pl.ds(z, count), 1 : TILES + 1]
            for z, count in groups
        ]
        value = jnp.dot(
            jnp.concatenate(cells).reshape(total * TILES * 8, 256),
            shift_ref[...],
            preferred_element_type=jnp.float32,
        )
        slopes[0:total] = value.astype(BF).reshape(total, TILES, 8, 512)
        for z, count in groups:
            mid = [src[z + k, 1] for k in range(count)]
            state.append((mid, [mid[k] - src[z + k, 0] for k in range(count)]))
        first, last = {}, {}
        for j in range(TILES):
            for g, (z, count) in enumerate(groups):
                mid, before = state[g]
                right = [src[z + k, j + 2] for k in range(count)]
                after = [right[k] - mid[k] for k in range(count)]
                column = [src[z - 1, j + 1]] + mid + [src[z + count, j + 1]]
                steps = [column[k + 1] - column[k] for k in range(count + 1)]
                for k in range(count):
                    at = z + k
                    old = old_ref[at, j]
                    change_x = axp[at, j] * after[k] - axm[at, j] * before[k]
                    change_z = azp[at, j] * steps[k + 1] - azm[at, j] * steps[k]
                    place = sum(size for _, size in groups[:g]) + k
                    change_y = (
                        ayp[at, j] * slopes[place, j, :, :256]
                        + aym[at, j] * slopes[place, j, :, 256:]
                    )
                    change = (change_x + change_z) + change_y
                    new = old + change.astype(jnp.float32)
                    new_ref[at, j] = new
                    short = new.astype(BF)
                    dst[at, j + 1] = short
                    if keep is not None:
                        snaps_ref[keep[0], keep[1] + k, j] = short
                    if j == 0:
                        first[g, k] = new
                    last[g, k] = new
                state[g] = (right, after)
        for g, (z, count) in enumerate(groups):
            for k in range(count):
                left, right = ghosts(first[g, k], last[g, k])
                dst[z + k, 0] = left
                dst[z + k, TILES + 1] = right

    def step(t, src, dst, old_ref, new_ref):
        pairs = (9 - t) // 2

        @pl.when(inner == 1)
        def _():
            def both(k, carry):
                planes(
                    [(OWN - 2 - 2 * k, 2), (HIGH + 2 * k, 2)], src, dst, old_ref, new_ref, None
                )
                return carry

            lax.fori_loop(0, pairs, both, 0)

        @pl.when(inner == 0)
        def _():
            def one(k, carry):
                base = jnp.where(par_base == LOW, OWN - 2 - 2 * k, HIGH + 2 * k)
                planes([(base, 2)], src, dst, old_ref, new_ref, None)
                return carry

            lax.fori_loop(0, pairs, one, 0)

        def own(k, carry):
            planes([(OWN + OWN_STEP * k, OWN_STEP)], src, dst, old_ref, new_ref, (t - 1, OWN_STEP * k))
            return carry

        lax.fori_loop(0, 8 // OWN_STEP, own, 0)

    def two_steps(k, carry):
        step(2 * k + 1, even, odd, full, full_odd)
        step(2 * k + 2, odd, even, full_odd, full)
        return carry

    lax.fori_loop(0, SNAPS // 2, two_steps, 0)

    def project(jp, carry):
        for e in range(2):
            for part in range(2):
                data = snaps_ref[:, 4 * part : 4 * part + 4, jp * 2 + e]
                value = jnp.dot(
                    matrix_ref[...], data.reshape(256, 256), preferred_element_type=jnp.float32
                )
                wide[e, :, 4 * part : 4 * part + 4] = value.reshape(8, 4, 8, 256)
        rows = pl.ds(pl.multiple_of(jp * 16, 16), 16)
        for o in range(8):
            for half in range(2):
                parts = [
                    jnp.swapaxes(wide[e, o, :, :, half * 128 : half * 128 + 128], 0, 1)
                    for e in range(2)
                ]
                out_ref[o, half * 8 : half * 8 + 8, rows, :] = (
                    jnp.concatenate(parts, axis=1).astype(BF)
                )
        return carry

    lax.fori_loop(0, TILES // 2, project, 0)


def y_slopes():
    here = np.eye(128, dtype=np.float32)
    both = [np.kron(np.eye(2), np.roll(here, by, axis=1) - here) for by in (-1, 1)]
    return jnp.asarray(np.concatenate(both, axis=1), BF)


def evolve(ints, speeds, matrix, own, par):
    smem = pl.BlockSpec(memory_space=pltpu.SMEM)

    def stream(index):
        return pl.BlockSpec((32, None, 64, 128), lambda v: (0, index(v), 0, 0))

    def coef_array(planes=PLANES, tiles=TILES):
        return pltpu.VMEM((planes, tiles, 8, 256), BF)

    wide = jnp.kron(matrix, jnp.eye(32, dtype=jnp.float32)).astype(BF)
    return pl.pallas_call(
        evolve_kernel,
        name="evolve",
        grid=(VARS,),
        in_specs=[
            smem, smem, pl.BlockSpec((256, 256), lambda v: (0, 0)),
            pl.BlockSpec((256, 512), lambda v: (0, 0)),
            stream(lambda v: 0), stream(lambda v: 0), stream(lambda v: 6),
            stream(lambda v: v + 1), stream(lambda v: v + 1),
            stream(lambda v: jnp.minimum(v + 7, 8)), stream(lambda v: jnp.maximum(v + 4, 6)),
        ],
        out_specs=pl.BlockSpec((8, None, 16, 128, 128), lambda v: (0, v, 0, 0, 0)),
        out_shape=jax.ShapeDtypeStruct((8, VARS, 16, 128, 128), BF),
        scratch_shapes=[
            pltpu.VMEM((2, 8, 8, 8, 256), jnp.float32),
            pltpu.VMEM((8, TILES, 8, 512), BF),
            pltpu.VMEM((SNAPS, 8, TILES, 8, 256), BF),
            pltpu.VMEM((PLANES, TILES, 8, 256), jnp.float32),
            pltpu.VMEM((PLANES, TILES, 8, 256), jnp.float32),
            coef_array(tiles=TILES + 2), coef_array(tiles=TILES + 2), coef_array(tiles=TILES + 1),
            coef_array(), coef_array(), coef_array(PLANES + 1),
            coef_array(), coef_array(), coef_array(),
            coef_array(), coef_array(), coef_array(),
        ],
        compiler_params=pltpu.CompilerParams(vmem_limit_bytes=66_000_000),
        cost_estimate=pl.CostEstimate(
            flops=400_000_000_000, bytes_accessed=40_000_000, transcendentals=0
        ),
    )(ints, speeds, wide, y_slopes(), own, par, own, own, par, own, par)


def ring_shift(axis_of_core, by):
    pairs = []
    for core in range(2):
        for y in range(4):
            for x in range(4):
                to = ((y + by) % 4, x) if axis_of_core[core] == "y" else (y, (x + by) % 4)
                pairs.append((core * 16 + y * 4 + x, core * 16 + to[0] * 4 + to[1]))
    return lambda value: lax.ppermute(value, ("grp_1", "dev_1", "dev_2"), pairs)


def swap_cores(value):
    return lax.ppermute(value, "grp_1", [(0, 1), (1, 0)])


SIDE = 24


def local_kernel(
    ints, speeds, weights, fields, final_ref, corr_ref,
    qa, qb, nx, nzp, nzm, nyp, nym, diag, snap,
):
    low, high = ints[0], ints[1]
    row = lax.broadcasted_iota(jnp.int32, (SIDE, 128), 0)
    mask = ((row >= ints[2]) & (row < ints[3])).astype(jnp.float32)
    rates = [[0.5 * speeds[v * 3 + d] for d in range(3)] for v in range(VARS)]

    def up(value):
        return pltpu.roll(value, SIDE - 1, axis=0)

    def down(value):
        return pltpu.roll(value, 1, axis=0)

    def faces(x, carry):
        mid = fields[0, x]
        right = (mid + fields[0, x + 1]) * 0.5
        left = (mid + fields[0, x - 1]) * 0.5
        above = (mid + up(mid)) * 0.5
        below = (mid + down(mid)) * 0.5
        ahead = (mid + pltpu.roll(mid, 127, axis=1)) * 0.5
        behind = (mid + pltpu.roll(mid, 1, axis=1)) * 0.5
        nx[x + 1] = right
        nx[x] = left
        nzp[x], nzm[x], nyp[x], nym[x] = above, below, ahead, behind
        diag[x] = 1.0 - ((right + left) + (above + below) + (ahead + behind))
        return carry

    lax.fori_loop(1, SIDE - 1, faces, 0)
    for v in range(VARS):
        qa[v] = fields[v + 1]
        qb[v] = fields[v + 1]

    def step(t, src, dst):
        def one(x, carry):
            for v in range(VARS):
                hx, hz, hy = rates[v]
                mid = src[v, x]
                new = (
                    diag[x] * mid
                    + ((nx[x + 1] - hx) * src[v, x + 1] + (nx[x] + hx) * src[v, x - 1])
                    + ((nzp[x] - hz) * up(mid) + (nzm[x] + hz) * down(mid))
                    + (
                        (nyp[x] - hy) * pltpu.roll(mid, 127, axis=1)
                        + (nym[x] + hy) * pltpu.roll(mid, 1, axis=1)
                    )
                )
                dst[v, x] = new * mask
            return carry

        lax.fori_loop(jnp.maximum(t, low), jnp.minimum(SIDE - t, high), one, 0)
        for v in range(VARS):
            for x in range(8):
                snap[t - 1, v, x] = dst[v, 8 + x, 8:16, :].astype(BF).astype(jnp.float32)

    def two_steps(k, carry):
        step(2 * k + 1, qa, qb)
        step(2 * k + 2, qb, qa)
        return carry

    lax.fori_loop(0, SNAPS // 2, two_steps, 0)
    for v in range(VARS):
        for x in range(8):
            final_ref[v, x] = qa[v, 8 + x, 8:16, :]

    corr_ref[...] = jnp.zeros_like(corr_ref)

    def correlate(v, carry):
        weight = weights[v]
        sums = [jnp.zeros((8, 128), jnp.float32)] * len(PAIRS)
        for x in range(8):
            vals = [snap[t, v, x] for t in range(SNAPS)]
            for n, (a, b) in enumerate(PAIRS):
                sums[n] = sums[n] + vals[a] * vals[b]
        for n in range(len(PAIRS)):
            corr_ref[n] += weight * sums[n]
        return carry

    lax.fori_loop(0, VARS, correlate, 0)


def local_steps(ints, speeds, weights, fields):
    smem = pl.BlockSpec(memory_space=pltpu.SMEM)
    vmem = pl.BlockSpec(memory_space=pltpu.VMEM)
    cube = pltpu.VMEM((SIDE, SIDE, 128), jnp.float32)
    cubes = pltpu.VMEM((VARS, SIDE, SIDE, 128), jnp.float32)
    return pl.pallas_call(
        local_kernel,
        name="local",
        in_specs=[smem, smem, smem, vmem],
        out_specs=[vmem, vmem],
        out_shape=[
            jax.ShapeDtypeStruct((VARS, 8, 8, 128), jnp.float32),
            jax.ShapeDtypeStruct((len(PAIRS), 8, 128), jnp.float32),
        ],
        scratch_shapes=[
            cubes, cubes, pltpu.VMEM((SIDE + 1, SIDE, 128), jnp.float32),
            cube, cube, cube, cube, cube,
            pltpu.VMEM((SNAPS, VARS, 8, 8, 128), jnp.float32),
        ],
        compiler_params=pltpu.CompilerParams(vmem_limit_bytes=24_000_000),
        cost_estimate=pl.CostEstimate(
            flops=4_000_000_000, bytes_accessed=6_000_000, transcendentals=0
        ),
    )(ints, speeds, weights, fields)


def local_ints():
    own = lax.axis_index(DEV)
    grp = lax.axis_index(GRP)
    bounds = [
        jnp.where(own == 0, 8, 0),
        jnp.where(own == 31, 16, SIDE),
        jnp.where(grp == 0, 8, 0),
        jnp.where(grp == 3, 16, SIDE),
    ]
    return jnp.stack(bounds).astype(jnp.int32)


def ring_sum(value, axes):
    one, two, three = (
        lax.ppermute(value, axes, [(i, (i + by) % 4) for i in range(4)]) for by in (1, 2, 3)
    )
    return (value + two) + (one + three)


def communicate(initial_state, viscosity, speeds, energy_weights):
    fields = jnp.concatenate([viscosity[None], initial_state])
    state = fields.astype(BF).reshape(VARS + 1, 64, 128)
    near = lax.ppermute(state[:3], GRP, [(2, 1), (1, 2)])
    far = lax.ppermute(state[3:], GRP, [(2, 0), (1, 3)])
    third = lax.ppermute(fields, GRP, [(1, 2), (2, 1)])
    par = swap_cores(fields)
    block = jnp.concatenate([state, near + far])
    other = lax.ppermute(block, "dev_0", [(0, 1), (1, 0)])

    odd = lax.axis_index("grp_1") == 1
    column = jnp.concatenate(
        [jnp.where(odd, par, third), fields, jnp.where(odd, third, par)], axis=2
    )
    up = [(i, i + 1) for i in range(31)]
    before_x = lax.ppermute(column, DEV, up)
    after_x = lax.ppermute(column, DEV, [(b, a) for a, b in up])
    cube = jnp.concatenate([before_x, column, after_x], axis=1)

    pair = jnp.stack([block, other])
    near_axis = [ring_shift(("y", "x"), by) for by in (-1, 2, 1)]
    first = jnp.stack([pair] + [shift(pair) for shift in near_axis])
    first, cube = lax.optimization_barrier((first, cube))
    forward, back = ring_shift(("x", "y"), 1), ring_shift(("x", "y"), -1)
    before, after = forward(first), back(first)
    final, corr = local_steps(local_ints(), speeds, energy_weights, cube)
    sums = jnp.sum(corr, axis=(1, 2)) / CELLS
    before, after, sums = lax.optimization_barrier((before, after, sums))
    half_before, half_after = forward(before[:2]), back(after[2:])
    sums = ring_sum(ring_sum(sums, "dev_2"), "dev_1")
    half_before, half_after, sums = lax.optimization_barrier((half_before, half_after, sums))
    across = jnp.concatenate([half_before, half_after])
    own = jnp.stack([first, after, across, before]).reshape(32, 9, 64, 128)
    partner = swap_cores(own)
    sums = ring_sum(sums, ("grp_0", "dev_0"))
    sums = sums + swap_cores(sums)
    return own, partner, final, sums


def layout_ints():
    h, c, l, y, x = (lax.axis_index(axis) for axis in GRP_DEV)
    d = jnp.arange(32)
    to_l, to_y, to_x = (d // 16 + l) % 2, (d // 4 - y) % 4, (d - x) % 4

    def slots(core):
        outer = jnp.where(core == 0, to_x, to_y)
        return outer * 8 + jnp.where(core == 0, to_y, to_x) * 2 + to_l

    inner = (h != c).astype(jnp.int32)
    par_base = jnp.where(c == 1, LOW, HIGH)
    scalars = [par_base, LOW + HIGH - par_base, inner]
    return jnp.concatenate([slots(c), slots(1 - c), jnp.stack(scalars)]).astype(jnp.int32)


def body(initial_state, viscosity, speeds, energy_weights, block_index, block_offset):
    speeds = speeds.reshape(-1)
    own, par, final, sums = communicate(initial_state, viscosity, speeds, energy_weights)
    order = [[PAIRS.index((min(a, b), max(a, b))) for b in range(SNAPS)] for a in range(SNAPS)]
    corr_matrix = sums[jnp.array(order)]
    coef = block_coefficients(block_index, block_offset)
    own_coef = lax.dynamic_slice_in_dim(coef, lax.axis_index(DEV) * 2, 2, 0)
    energy, matrix = mode_matrix(own_coef, corr_matrix)
    modes = evolve(layout_ints(), speeds, matrix.reshape(8, SNAPS), own, par)
    return final, modes.reshape(2, BLOCKS, 2, VARS, 256, 8, 128), energy


def solution(mesh):
    torus = Mesh(mesh.devices.reshape(2, 2, 2, 4, 4), GRP_DEV)
    in_specs = (P(None, DEV, GRP, None), P(DEV, GRP, None), P(), P(), P(), P())
    out_specs = (P(None, DEV, GRP, None), P(DEV, None, None, None, None, GRP, None), P(DEV))
    return jax.shard_map(body, mesh=torus, in_specs=in_specs, out_specs=out_specs, check_vma=False)
```

```python
import math

import jax
import jax.numpy as jnp
import numpy as np
from jax import lax
from jax.experimental import pallas as pl
from jax.experimental.pallas import tpu as pltpu
from jax.sharding import Mesh
from jax.sharding import PartitionSpec as P

VARS = 5
FREQS = 64
BLOCKS = 2
SNAPS = 8
GRP_DEV = ("grp_0", "grp_1", "dev_0", "dev_1", "dev_2")
GRP = ("grp_0", "grp_1")
DEV = ("dev_0", "dev_1", "dev_2")
CELLS = 256 * 32 * 128

TILES = 16
PLANES = 26
LOW, OWN, HIGH = 1, 9, 17
PAIRS = [(a, b) for a in range(SNAPS) for b in range(a, SNAPS)]
BF = jnp.bfloat16


def block_coefficients(block_index, block_offset):
    frequency = jnp.arange(FREQS)
    distance = block_index - block_offset[:, None]
    angles = (frequency[:, None, None] * distance[None]).astype(jnp.float32) * (math.pi / FREQS)
    length = block_index.shape[1]
    window = jnp.sin(math.pi * (jnp.arange(length).astype(jnp.float32) + 0.5) / length) ** 2
    onehot = (block_index[:, :, None] == jnp.arange(SNAPS)[None, None, :]).astype(jnp.float32)
    cosine = jnp.sum((window * jnp.cos(angles))[..., None] * onehot[None], axis=2)
    sine = -jnp.sum((window * jnp.sin(angles))[..., None] * onehot[None], axis=2)
    return jnp.stack([cosine, sine], axis=2)


def mode_matrix(coef, corr):
    def form(a, b):
        return jnp.sum(a[:, :, None] * corr[None] * b[:, None, :], axis=(1, 2))

    a0, b0, a1, b1 = coef[:, 0, 0], coef[:, 0, 1], coef[:, 1, 0], coef[:, 1, 1]
    g00 = form(a0, a0) + form(b0, b0)
    g11 = form(a1, a1) + form(b1, b1)
    gre = form(a0, a1) + form(b0, b1)
    gim = form(a0, b1) - form(b0, a1)
    middle = (g00 + g11) * 0.5
    radius = jnp.sqrt(((g00 - g11) * 0.5) ** 2 + gre**2 + gim**2)
    low = middle - radius
    total = g00 + g11 + 1e-06
    k0, k1 = ((g00 - low) / total)[:, None], ((g11 - low) / total)[:, None]
    cr, ci = (gre / total)[:, None], (gim / total)[:, None]
    rows = [
        a0 * k0 + a1 * cr + b1 * ci,
        b0 * k0 + b1 * cr - a1 * ci,
        a0 * cr - b0 * ci + a1 * k1,
        b0 * cr + a0 * ci + b1 * k1,
    ]
    return middle + radius, jnp.stack(rows, axis=1)


def by_half(fn, *values):
    parts = [fn(*[v[:, half * 128 : half * 128 + 128] for v in values]) for half in range(2)]
    return jnp.concatenate(parts, axis=1)


def ghosts(first, last):
    place = lax.broadcasted_iota(jnp.int32, (8, 128), 0)
    low, high = (pltpu.roll(last[:, k : k + 128], 1, axis=0) for k in (0, 128))
    left = jnp.concatenate(
        [jnp.where(place == 0, 0.0, low), jnp.where(place == 0, low, high)], axis=1
    )
    low, high = (pltpu.roll(first[:, k : k + 128], 7, axis=0) for k in (0, 128))
    right = jnp.concatenate(
        [jnp.where(place == 7, high, low), jnp.where(place == 7, 0.0, high)], axis=1
    )
    return left.astype(BF), right.astype(BF)


def y_next(value):
    return by_half(lambda part: pltpu.roll(part, 127, axis=1), value)


def y_last(value):
    return by_half(lambda part: pltpu.roll(part, 1, axis=1), value)


def evolve_kernel(
    ints, speeds, matrix_ref, shift_ref, nu_own, nu_par, nu_third, q_own, q_par, q_ta, q_tb,
    out_ref, wide, slopes, snaps_ref, full, full_odd, even, odd, nx, ny, nym, nz, axp, axm, ayp, aym, azp, azm,
):
    var = pl.program_id(0)
    par_base, third_base, inner = ints[64], ints[65], ints[66]

    def load_section(src, table, base):
        for dl in range(2):
            def pair(ip, carry):
                rows = pl.ds(pl.multiple_of(ip * 16, 16), 16)
                halves = []
                for half in range(2):
                    blocks = [
                        src[ints[table + (half * 8 + s) * 2 + dl], rows, :].astype(jnp.float32)
                        for s in range(8)
                    ]
                    grid = jnp.stack(blocks).reshape(8, 2, 8, 128)
                    halves.append([jnp.swapaxes(grid[:, i], 0, 1) for i in range(2)])
                for i in range(2):
                    slot = dl * 8 + ip * 2 + i
                    for z in range(8):
                        val = jnp.concatenate([halves[0][i][z], halves[1][i][z]], axis=1)
                        full[base + z, slot] = val
                        even[base + z, slot + 1] = val.astype(BF)
                return carry

            lax.fori_loop(0, 4, pair, 0)

        def edge(z, carry):
            left, right = ghosts(full[base + z, 0], full[base + z, TILES - 1])
            even[base + z, 0] = left
            even[base + z, TILES + 1] = right
            return carry

        lax.fori_loop(0, 8, edge, 0)

    def load_all(own, par, third):
        load_section(own, 0, OWN)
        load_section(par, 32, par_base)

        @pl.when(inner == 1)
        def _():
            third()

    @pl.when(var == 0)
    def _():
        @pl.when(inner == 0)
        def _():
            def clear(k, carry):
                even[third_base + k] = jnp.zeros((TILES + 2, 8, 256), BF)
                odd[third_base + k] = jnp.zeros((TILES + 2, 8, 256), BF)
                full[third_base + k] = jnp.zeros((TILES, 8, 256), jnp.float32)
                full_odd[third_base + k] = jnp.zeros((TILES, 8, 256), jnp.float32)
                return carry

            lax.fori_loop(0, 8, clear, 0)

            def still(k, carry):
                for coef in (axp, axm, ayp, aym, azp, azm):
                    coef[third_base + k] = jnp.zeros((TILES, 8, 256), BF)
                return carry

            lax.fori_loop(0, 8, still, 0)

        load_all(nu_own, nu_par, lambda: load_section(nu_third, 0, third_base))

        def faces(z, carry):
            def nu(plane, slot):
                return even[plane, slot].astype(jnp.float32)

            mid = full[z, 0]
            nx[z, 0] = ((nu(z, 0) + mid) * 0.5).astype(BF)
            for j in range(TILES):
                right = nu(z, j + 2)
                face_y = (mid + y_next(mid)) * 0.5
                nx[z, j + 1] = ((mid + right) * 0.5).astype(BF)
                nz[z + 1, j] = ((mid + full[z + 1, j]) * 0.5).astype(BF)
                nz[z, j] = ((mid + full[z - 1, j]) * 0.5).astype(BF)
                ny[z, j] = face_y.astype(BF)
                nym[z, j] = y_last(face_y).astype(BF)
                mid = right
            return carry

        lax.fori_loop(2, PLANES - 2, faces, 0)

    def third():
        @pl.when(var < 2)
        def _():
            load_section(q_ta, 0, third_base)

        @pl.when(var >= 2)
        def _():
            load_section(q_tb, 32, third_base)

    load_all(q_own, q_par, third)

    hx, hz, hy = ((0.5 * speeds[var * 3 + d]).astype(BF) for d in range(3))

    def coefs(z, carry):
        for j in range(TILES):
            axp[z, j] = nx[z, j + 1] - hx
            axm[z, j] = nx[z, j] + hx
            azp[z, j] = nz[z + 1, j] - hz
            azm[z, j] = nz[z, j] + hz
            ayp[z, j] = ny[z, j] - hy
            aym[z, j] = nym[z, j] + hy
        return carry

    outer = inner == 0
    lax.fori_loop(
        jnp.where(outer & (third_base == LOW), OWN, 2),
        jnp.where(outer & (third_base == HIGH), HIGH, PLANES - 2),
        coefs,
        0,
    )

    def planes(groups, src, dst, old_ref, new_ref, keep):
        state = []
        total = sum(count for _, count in groups)
        cells = [
            src[z : z + count, 1 : TILES + 1] if isinstance(z, int)
            else src[pl.ds(z, count), 1 : TILES + 1]
            for z, count in groups
        ]
        value = jnp.dot(
            jnp.concatenate(cells).reshape(total * TILES * 8, 256),
            shift_ref[...],
            preferred_element_type=jnp.float32,
        )
        slopes[0:total] = value.astype(BF).reshape(total, TILES, 8, 512)
        for z, count in groups:
            mid = [src[z + k, 1] for k in range(count)]
            state.append((mid, [mid[k] - src[z + k, 0] for k in range(count)]))
        first, last = {}, {}
        for j in range(TILES):
            for g, (z, count) in enumerate(groups):
                mid, before = state[g]
                right = [src[z + k, j + 2] for k in range(count)]
                after = [right[k] - mid[k] for k in range(count)]
                column = [src[z - 1, j + 1]] + mid + [src[z + count, j + 1]]
                steps = [column[k + 1] - column[k] for k in range(count + 1)]
                for k in range(count):
                    at = z + k
                    old = old_ref[at, j]
                    change_x = axp[at, j] * after[k] - axm[at, j] * before[k]
                    change_z = azp[at, j] * steps[k + 1] - azm[at, j] * steps[k]
                    place = sum(size for _, size in groups[:g]) + k
                    change_y = (
                        ayp[at, j] * slopes[place, j, :, :256]
                        + aym[at, j] * slopes[place, j, :, 256:]
                    )
                    change = (change_x + change_z) + change_y
                    new = old + change.astype(jnp.float32)
                    new_ref[at, j] = new
                    short = new.astype(BF)
                    dst[at, j + 1] = short
                    if keep is not None:
                        snaps_ref[keep[0], keep[1] + k, j] = short
                    if j == 0:
                        first[g, k] = new
                    last[g, k] = new
                state[g] = (right, after)
        for g, (z, count) in enumerate(groups):
            for k in range(count):
                left, right = ghosts(first[g, k], last[g, k])
                dst[z + k, 0] = left
                dst[z + k, TILES + 1] = right

    for t in range(1, SNAPS + 1):
        refs = (even, odd, full, full_odd) if t % 2 else (odd, even, full_odd, full)
        deep = 8 - t
        if deep:
            planes([(OWN - deep, deep), (HIGH, deep)], *refs, None)
        planes([(OWN, 8)], *refs, (t - 1, 0))

    def project(jp, carry):
        for e in range(2):
            for part in range(2):
                data = snaps_ref[:, 4 * part : 4 * part + 4, jp * 2 + e]
                value = jnp.dot(
                    matrix_ref[...], data.reshape(256, 256), preferred_element_type=jnp.float32
                )
                wide[e, :, 4 * part : 4 * part + 4] = value.reshape(8, 4, 8, 256)
        rows = pl.ds(pl.multiple_of(jp * 16, 16), 16)
        for o in range(8):
            for half in range(2):
                parts = [
                    jnp.swapaxes(wide[e, o, :, :, half * 128 : half * 128 + 128], 0, 1)
                    for e in range(2)
                ]
                out_ref[o, half * 8 : half * 8 + 8, rows, :] = (
                    jnp.concatenate(parts, axis=1).astype(BF)
                )
        return carry

    lax.fori_loop(0, TILES // 2, project, 0)


def y_slopes():
    here = np.eye(128, dtype=np.float32)
    both = [np.kron(np.eye(2), np.roll(here, by, axis=1) - here) for by in (-1, 1)]
    return jnp.asarray(np.concatenate(both, axis=1), BF)


def evolve(ints, speeds, matrix, own, par):
    smem = pl.BlockSpec(memory_space=pltpu.SMEM)

    def stream(index):
        return pl.BlockSpec((32, None, 64, 128), lambda v: (0, index(v), 0, 0))

    def coef_array(planes=PLANES, tiles=TILES):
        return pltpu.VMEM((planes, tiles, 8, 256), BF)

    wide = jnp.kron(matrix, jnp.eye(32, dtype=jnp.float32)).astype(BF)
    return pl.pallas_call(
        evolve_kernel,
        name="evolve",
        grid=(VARS,),
        in_specs=[
            smem, smem, pl.BlockSpec((256, 256), lambda v: (0, 0)),
            pl.BlockSpec((256, 512), lambda v: (0, 0)),
            stream(lambda v: 0), stream(lambda v: 0), stream(lambda v: 6),
            stream(lambda v: v + 1), stream(lambda v: v + 1),
            stream(lambda v: jnp.minimum(v + 7, 8)), stream(lambda v: jnp.maximum(v + 4, 6)),
        ],
        out_specs=pl.BlockSpec((8, None, 16, 128, 128), lambda v: (0, v, 0, 0, 0)),
        out_shape=jax.ShapeDtypeStruct((8, VARS, 16, 128, 128), BF),
        scratch_shapes=[
            pltpu.VMEM((2, 8, 8, 8, 256), jnp.float32),
            pltpu.VMEM((14, TILES, 8, 512), BF),
            pltpu.VMEM((SNAPS, 8, TILES, 8, 256), BF),
            pltpu.VMEM((PLANES, TILES, 8, 256), jnp.float32),
            pltpu.VMEM((PLANES, TILES, 8, 256), jnp.float32),
            coef_array(tiles=TILES + 2), coef_array(tiles=TILES + 2), coef_array(tiles=TILES + 1),
            coef_array(), coef_array(), coef_array(PLANES + 1),
            coef_array(), coef_array(), coef_array(),
            coef_array(), coef_array(), coef_array(),
        ],
        compiler_params=pltpu.CompilerParams(vmem_limit_bytes=66_000_000),
        cost_estimate=pl.CostEstimate(
            flops=400_000_000_000, bytes_accessed=40_000_000, transcendentals=0
        ),
    )(ints, speeds, wide, y_slopes(), own, par, own, own, par, own, par)


def ring_shift(axis_of_core, by):
    pairs = []
    for core in range(2):
        for y in range(4):
            for x in range(4):
                to = ((y + by) % 4, x) if axis_of_core[core] == "y" else (y, (x + by) % 4)
                pairs.append((core * 16 + y * 4 + x, core * 16 + to[0] * 4 + to[1]))
    return lambda value: lax.ppermute(value, ("grp_1", "dev_1", "dev_2"), pairs)


def swap_cores(value):
    return lax.ppermute(value, "grp_1", [(0, 1), (1, 0)])


SIDE = 24


def local_kernel(
    ints, speeds, weights, fields, final_ref, corr_ref,
    qa, qb, nx, nzp, nzm, nyp, nym, diag, snap,
):
    low, high = ints[0], ints[1]
    row = lax.broadcasted_iota(jnp.int32, (SIDE, 128), 0)
    mask = ((row >= ints[2]) & (row < ints[3])).astype(jnp.float32)
    rates = [[0.5 * speeds[v * 3 + d] for d in range(3)] for v in range(VARS)]

    def up(value):
        return pltpu.roll(value, SIDE - 1, axis=0)

    def down(value):
        return pltpu.roll(value, 1, axis=0)

    def faces(x, carry):
        mid = fields[0, x]
        right = (mid + fields[0, x + 1]) * 0.5
        left = (mid + fields[0, x - 1]) * 0.5
        above = (mid + up(mid)) * 0.5
        below = (mid + down(mid)) * 0.5
        ahead = (mid + pltpu.roll(mid, 127, axis=1)) * 0.5
        behind = (mid + pltpu.roll(mid, 1, axis=1)) * 0.5
        nx[x + 1] = right
        nx[x] = left
        nzp[x], nzm[x], nyp[x], nym[x] = above, below, ahead, behind
        diag[x] = 1.0 - ((right + left) + (above + below) + (ahead + behind))
        return carry

    lax.fori_loop(1, SIDE - 1, faces, 0)
    for v in range(VARS):
        qa[v] = fields[v + 1]
        qb[v] = fields[v + 1]

    def step(t, src, dst):
        def one(x, carry):
            for v in range(VARS):
                hx, hz, hy = rates[v]
                mid = src[v, x]
                new = (
                    diag[x] * mid
                    + ((nx[x + 1] - hx) * src[v, x + 1] + (nx[x] + hx) * src[v, x - 1])
                    + ((nzp[x] - hz) * up(mid) + (nzm[x] + hz) * down(mid))
                    + (
                        (nyp[x] - hy) * pltpu.roll(mid, 127, axis=1)
                        + (nym[x] + hy) * pltpu.roll(mid, 1, axis=1)
                    )
                )
                dst[v, x] = new * mask
            return carry

        lax.fori_loop(jnp.maximum(t, low), jnp.minimum(SIDE - t, high), one, 0)
        for v in range(VARS):
            for x in range(8):
                snap[t - 1, v, x] = dst[v, 8 + x, 8:16, :].astype(BF).astype(jnp.float32)

    def two_steps(k, carry):
        step(2 * k + 1, qa, qb)
        step(2 * k + 2, qb, qa)
        return carry

    lax.fori_loop(0, SNAPS // 2, two_steps, 0)
    for v in range(VARS):
        for x in range(8):
            final_ref[v, x] = qa[v, 8 + x, 8:16, :]

    corr_ref[...] = jnp.zeros_like(corr_ref)

    def correlate(v, carry):
        weight = weights[v]
        sums = [jnp.zeros((8, 128), jnp.float32)] * len(PAIRS)
        for x in range(8):
            vals = [snap[t, v, x] for t in range(SNAPS)]
            for n, (a, b) in enumerate(PAIRS):
                sums[n] = sums[n] + vals[a] * vals[b]
        for n in range(len(PAIRS)):
            corr_ref[n] += weight * sums[n]
        return carry

    lax.fori_loop(0, VARS, correlate, 0)


def local_steps(ints, speeds, weights, fields):
    smem = pl.BlockSpec(memory_space=pltpu.SMEM)
    vmem = pl.BlockSpec(memory_space=pltpu.VMEM)
    cube = pltpu.VMEM((SIDE, SIDE, 128), jnp.float32)
    cubes = pltpu.VMEM((VARS, SIDE, SIDE, 128), jnp.float32)
    return pl.pallas_call(
        local_kernel,
        name="local",
        in_specs=[smem, smem, smem, vmem],
        out_specs=[vmem, vmem],
        out_shape=[
            jax.ShapeDtypeStruct((VARS, 8, 8, 128), jnp.float32),
            jax.ShapeDtypeStruct((len(PAIRS), 8, 128), jnp.float32),
        ],
        scratch_shapes=[
            cubes, cubes, pltpu.VMEM((SIDE + 1, SIDE, 128), jnp.float32),
            cube, cube, cube, cube, cube,
            pltpu.VMEM((SNAPS, VARS, 8, 8, 128), jnp.float32),
        ],
        compiler_params=pltpu.CompilerParams(vmem_limit_bytes=24_000_000),
        cost_estimate=pl.CostEstimate(
            flops=4_000_000_000, bytes_accessed=6_000_000, transcendentals=0
        ),
    )(ints, speeds, weights, fields)


def local_ints():
    own = lax.axis_index(DEV)
    grp = lax.axis_index(GRP)
    bounds = [
        jnp.where(own == 0, 8, 0),
        jnp.where(own == 31, 16, SIDE),
        jnp.where(grp == 0, 8, 0),
        jnp.where(grp == 3, 16, SIDE),
    ]
    return jnp.stack(bounds).astype(jnp.int32)


def ring_sum(value, axes):
    one, two, three = (
        lax.ppermute(value, axes, [(i, (i + by) % 4) for i in range(4)]) for by in (1, 2, 3)
    )
    return (value + two) + (one + three)


def communicate(initial_state, viscosity, speeds, energy_weights):
    fields = jnp.concatenate([viscosity[None], initial_state])
    state = fields.astype(BF).reshape(VARS + 1, 64, 128)
    near = lax.ppermute(state[:3], GRP, [(2, 1), (1, 2)])
    far = lax.ppermute(state[3:], GRP, [(2, 0), (1, 3)])
    block = jnp.concatenate([state, near + far])
    block, fields = lax.optimization_barrier((block, fields))
    other = lax.ppermute(block, "dev_0", [(0, 1), (1, 0)])
    third = lax.ppermute(fields, GRP, [(1, 2), (2, 1)])
    par = swap_cores(fields)

    odd = lax.axis_index("grp_1") == 1
    column = jnp.concatenate(
        [jnp.where(odd, par, third), fields, jnp.where(odd, third, par)], axis=2
    )
    pair = jnp.stack([block, other])
    column, _ = lax.optimization_barrier((column, pair))
    near_axis = [ring_shift(("y", "x"), by) for by in (-1, 2, 1)]
    first = jnp.stack([pair] + [shift(pair) for shift in near_axis])
    up = [(i, i + 1) for i in range(31)]
    before_x = lax.ppermute(column, DEV, up)
    after_x = lax.ppermute(column, DEV, [(b, a) for a, b in up])
    cube = jnp.concatenate([before_x, column, after_x], axis=1)

    forward, back = ring_shift(("x", "y"), 1), ring_shift(("x", "y"), -1)
    before, after = forward(first), back(first)
    cube, _ = lax.optimization_barrier((cube, first))
    final, corr = local_steps(local_ints(), speeds, energy_weights, cube)
    sums = jnp.sum(corr, axis=(1, 2)) / CELLS
    before, after, sums = lax.optimization_barrier((before, after, sums))
    half_before, half_after = forward(before[:2]), back(after[2:])
    sums = ring_sum(ring_sum(sums, "dev_2"), "dev_1")
    half_before, half_after, sums = lax.optimization_barrier((half_before, half_after, sums))
    across = jnp.concatenate([half_before, half_after])
    own = jnp.stack([first, after, across, before]).reshape(32, 9, 64, 128)
    partner = swap_cores(own)
    sums = ring_sum(sums, ("grp_0", "dev_0"))
    sums = sums + swap_cores(sums)
    return own, partner, final, sums


def layout_ints():
    h, c, l, y, x = (lax.axis_index(axis) for axis in GRP_DEV)
    d = jnp.arange(32)
    to_l, to_y, to_x = (d // 16 + l) % 2, (d // 4 - y) % 4, (d - x) % 4

    def slots(core):
        outer = jnp.where(core == 0, to_x, to_y)
        return outer * 8 + jnp.where(core == 0, to_y, to_x) * 2 + to_l

    inner = (h != c).astype(jnp.int32)
    par_base = jnp.where(c == 1, LOW, HIGH)
    scalars = [par_base, LOW + HIGH - par_base, inner]
    return jnp.concatenate([slots(c), slots(1 - c), jnp.stack(scalars)]).astype(jnp.int32)


def body(initial_state, viscosity, speeds, energy_weights, block_index, block_offset):
    speeds = speeds.reshape(-1)
    own, par, final, sums = communicate(initial_state, viscosity, speeds, energy_weights)
    order = [[PAIRS.index((min(a, b), max(a, b))) for b in range(SNAPS)] for a in range(SNAPS)]
    corr_matrix = sums[jnp.array(order)]
    coef = block_coefficients(block_index, block_offset)
    own_coef = lax.dynamic_slice_in_dim(coef, lax.axis_index(DEV) * 2, 2, 0)
    energy, matrix = mode_matrix(own_coef, corr_matrix)
    modes = evolve(layout_ints(), speeds, matrix.reshape(8, SNAPS), own, par)
    return final, modes.reshape(2, BLOCKS, 2, VARS, 256, 8, 128), energy


def solution(mesh):
    torus = Mesh(mesh.devices.reshape(2, 2, 2, 4, 4), GRP_DEV)
    in_specs = (P(None, DEV, GRP, None), P(DEV, GRP, None), P(), P(), P(), P())
    out_specs = (P(None, DEV, GRP, None), P(DEV, None, None, None, None, GRP, None), P(DEV))
    return jax.shard_map(body, mesh=torus, in_specs=in_specs, out_specs=out_specs, check_vma=False)
```

```python
import math

import jax
import jax.numpy as jnp
import numpy as np
from jax import lax
from jax.experimental import pallas as pl
from jax.experimental.pallas import tpu as pltpu
from jax.sharding import Mesh
from jax.sharding import PartitionSpec as P

VARS = 5
FREQS = 64
BLOCKS = 2
SNAPS = 8
GRP_DEV = ("grp_0", "grp_1", "dev_0", "dev_1", "dev_2")
GRP = ("grp_0", "grp_1")
DEV = ("dev_0", "dev_1", "dev_2")
CELLS = 256 * 32 * 128

TILES = 16
PLANES = 26
LOW, OWN, HIGH = 1, 9, 17
PAIRS = [(a, b) for a in range(SNAPS) for b in range(a, SNAPS)]
BF = jnp.bfloat16


def block_coefficients(block_index, block_offset):
    frequency = jnp.arange(FREQS)
    distance = block_index - block_offset[:, None]
    angles = (frequency[:, None, None] * distance[None]).astype(jnp.float32) * (math.pi / FREQS)
    length = block_index.shape[1]
    window = jnp.sin(math.pi * (jnp.arange(length).astype(jnp.float32) + 0.5) / length) ** 2
    onehot = (block_index[:, :, None] == jnp.arange(SNAPS)[None, None, :]).astype(jnp.float32)
    cosine = jnp.sum((window * jnp.cos(angles))[..., None] * onehot[None], axis=2)
    sine = -jnp.sum((window * jnp.sin(angles))[..., None] * onehot[None], axis=2)
    return jnp.stack([cosine, sine], axis=2)


def mode_matrix(coef, corr):
    def form(a, b):
        return jnp.sum(a[:, :, None] * corr[None] * b[:, None, :], axis=(1, 2))

    a0, b0, a1, b1 = coef[:, 0, 0], coef[:, 0, 1], coef[:, 1, 0], coef[:, 1, 1]
    g00 = form(a0, a0) + form(b0, b0)
    g11 = form(a1, a1) + form(b1, b1)
    gre = form(a0, a1) + form(b0, b1)
    gim = form(a0, b1) - form(b0, a1)
    middle = (g00 + g11) * 0.5
    radius = jnp.sqrt(((g00 - g11) * 0.5) ** 2 + gre**2 + gim**2)
    low = middle - radius
    total = g00 + g11 + 1e-06
    k0, k1 = ((g00 - low) / total)[:, None], ((g11 - low) / total)[:, None]
    cr, ci = (gre / total)[:, None], (gim / total)[:, None]
    rows = [
        a0 * k0 + a1 * cr + b1 * ci,
        b0 * k0 + b1 * cr - a1 * ci,
        a0 * cr - b0 * ci + a1 * k1,
        b0 * cr + a0 * ci + b1 * k1,
    ]
    return middle + radius, jnp.stack(rows, axis=1)


def by_half(fn, *values):
    parts = [fn(*[v[:, half * 128 : half * 128 + 128] for v in values]) for half in range(2)]
    return jnp.concatenate(parts, axis=1)


def ghosts(first, last):
    place = lax.broadcasted_iota(jnp.int32, (8, 128), 0)
    low, high = (pltpu.roll(last[:, k : k + 128], 1, axis=0) for k in (0, 128))
    left = jnp.concatenate(
        [jnp.where(place == 0, 0.0, low), jnp.where(place == 0, low, high)], axis=1
    )
    low, high = (pltpu.roll(first[:, k : k + 128], 7, axis=0) for k in (0, 128))
    right = jnp.concatenate(
        [jnp.where(place == 7, high, low), jnp.where(place == 7, 0.0, high)], axis=1
    )
    return left.astype(BF), right.astype(BF)


def y_next(value):
    return by_half(lambda part: pltpu.roll(part, 127, axis=1), value)


def y_last(value):
    return by_half(lambda part: pltpu.roll(part, 1, axis=1), value)


def evolve_kernel(
    ints, speeds, matrix_ref, shift_ref, nu_own, nu_par, nu_third, q_own, q_par, q_ta, q_tb,
    out_ref, wide, slopes, snaps_ref, full, full_odd, even, odd, nx, ny, nym, nz, axp, axm, ayp, aym, azp, azm,
):
    var = pl.program_id(0)
    par_base, third_base, inner = ints[64], ints[65], ints[66]

    def load_section(src, table, base):
        for dl in range(2):
            def pair(ip, carry):
                rows = pl.ds(pl.multiple_of(ip * 16, 16), 16)
                halves = []
                for half in range(2):
                    blocks = [
                        src[ints[table + (half * 8 + s) * 2 + dl], rows, :].astype(jnp.float32)
                        for s in range(8)
                    ]
                    grid = jnp.stack(blocks).reshape(8, 2, 8, 128)
                    halves.append([jnp.swapaxes(grid[:, i], 0, 1) for i in range(2)])
                for i in range(2):
                    slot = dl * 8 + ip * 2 + i
                    for z in range(8):
                        val = jnp.concatenate([halves[0][i][z], halves[1][i][z]], axis=1)
                        full[base + z, slot] = val
                        even[base + z, slot + 1] = val.astype(BF)
                return carry

            lax.fori_loop(0, 4, pair, 0)

        def edge(z, carry):
            left, right = ghosts(full[base + z, 0], full[base + z, TILES - 1])
            even[base + z, 0] = left
            even[base + z, TILES + 1] = right
            return carry

        lax.fori_loop(0, 8, edge, 0)

    def load_all(own, par, third):
        load_section(own, 0, OWN)
        load_section(par, 32, par_base)

        @pl.when(inner == 1)
        def _():
            third()

    @pl.when(var == 0)
    def _():
        @pl.when(inner == 0)
        def _():
            def clear(k, carry):
                even[third_base + k] = jnp.zeros((TILES + 2, 8, 256), BF)
                odd[third_base + k] = jnp.zeros((TILES + 2, 8, 256), BF)
                full[third_base + k] = jnp.zeros((TILES, 8, 256), jnp.float32)
                full_odd[third_base + k] = jnp.zeros((TILES, 8, 256), jnp.float32)
                return carry

            lax.fori_loop(0, 8, clear, 0)

            def still(k, carry):
                for coef in (axp, axm, ayp, aym, azp, azm):
                    coef[third_base + k] = jnp.zeros((TILES, 8, 256), BF)
                return carry

            lax.fori_loop(0, 8, still, 0)

        load_all(nu_own, nu_par, lambda: load_section(nu_third, 0, third_base))

        def faces(z, carry):
            def nu(plane, slot):
                return even[plane, slot].astype(jnp.float32)

            mid = full[z, 0]
            nx[z, 0] = ((nu(z, 0) + mid) * 0.5).astype(BF)
            for j in range(TILES):
                right = nu(z, j + 2)
                face_y = (mid + y_next(mid)) * 0.5
                nx[z, j + 1] = ((mid + right) * 0.5).astype(BF)
                nz[z + 1, j] = ((mid + full[z + 1, j]) * 0.5).astype(BF)
                nz[z, j] = ((mid + full[z - 1, j]) * 0.5).astype(BF)
                ny[z, j] = face_y.astype(BF)
                nym[z, j] = y_last(face_y).astype(BF)
                mid = right
            return carry

        lax.fori_loop(2, PLANES - 2, faces, 0)

    def third():
        @pl.when(var < 2)
        def _():
            load_section(q_ta, 0, third_base)

        @pl.when(var >= 2)
        def _():
            load_section(q_tb, 32, third_base)

    load_all(q_own, q_par, third)

    hx, hz, hy = ((0.5 * speeds[var * 3 + d]).astype(BF) for d in range(3))

    def coefs(z, carry):
        for j in range(TILES):
            axp[z, j] = nx[z, j + 1] - hx
            axm[z, j] = nx[z, j] + hx
            azp[z, j] = nz[z + 1, j] - hz
            azm[z, j] = nz[z, j] + hz
            ayp[z, j] = ny[z, j] - hy
            aym[z, j] = nym[z, j] + hy
        return carry

    outer = inner == 0
    lax.fori_loop(
        jnp.where(outer & (third_base == LOW), OWN, 2),
        jnp.where(outer & (third_base == HIGH), HIGH, PLANES - 2),
        coefs,
        0,
    )

    def planes(groups, src, dst, old_ref, new_ref, keep):
        state = []
        total = sum(count for _, count in groups)
        cells = [
            src[z : z + count, 1 : TILES + 1] if isinstance(z, int)
            else src[pl.ds(z, count), 1 : TILES + 1]
            for z, count in groups
        ]
        value = jnp.dot(
            jnp.concatenate(cells).reshape(total * TILES * 8, 256),
            shift_ref[...],
            preferred_element_type=jnp.float32,
        )
        slopes[0:total] = value.astype(BF).reshape(total, TILES, 8, 512)
        for z, count in groups:
            mid = [src[z + k, 1] for k in range(count)]
            state.append((mid, [mid[k] - src[z + k, 0] for k in range(count)]))
        first, last = {}, {}
        for j in range(TILES):
            for g, (z, count) in enumerate(groups):
                mid, before = state[g]
                right = [src[z + k, j + 2] for k in range(count)]
                after = [right[k] - mid[k] for k in range(count)]
                column = [src[z - 1, j + 1]] + mid + [src[z + count, j + 1]]
                steps = [column[k + 1] - column[k] for k in range(count + 1)]
                for k in range(count):
                    at = z + k
                    old = old_ref[at, j]
                    change_x = axp[at, j] * after[k] - axm[at, j] * before[k]
                    change_z = azp[at, j] * steps[k + 1] - azm[at, j] * steps[k]
                    place = sum(size for _, size in groups[:g]) + k
                    change_y = (
                        ayp[at, j] * slopes[place, j, :, :256]
                        + aym[at, j] * slopes[place, j, :, 256:]
                    )
                    change = (change_x + change_z) + change_y
                    new = old + change.astype(jnp.float32)
                    new_ref[at, j] = new
                    short = new.astype(BF)
                    dst[at, j + 1] = short
                    if keep is not None:
                        snaps_ref[keep[0], keep[1] + k, j] = short
                    if j == 0:
                        first[g, k] = new
                    last[g, k] = new
                state[g] = (right, after)
        for g, (z, count) in enumerate(groups):
            for k in range(count):
                left, right = ghosts(first[g, k], last[g, k])
                dst[z + k, 0] = left
                dst[z + k, TILES + 1] = right

    for t in range(1, SNAPS + 1):
        refs = (even, odd, full, full_odd) if t % 2 else (odd, even, full_odd, full)
        deep = 8 - t
        if deep:
            planes([(OWN - deep, deep), (HIGH, deep)], *refs, None)
        planes([(OWN, 8)], *refs, (t - 1, 0))

    def project(jp, carry):
        for e in range(2):
            for part in range(2):
                data = snaps_ref[:, 4 * part : 4 * part + 4, jp * 2 + e]
                value = jnp.dot(
                    matrix_ref[...], data.reshape(256, 256), preferred_element_type=jnp.float32
                )
                wide[e, :, 4 * part : 4 * part + 4] = value.reshape(8, 4, 8, 256)
        rows = pl.ds(pl.multiple_of(jp * 16, 16), 16)
        for o in range(8):
            for half in range(2):
                parts = [
                    jnp.swapaxes(wide[e, o, :, :, half * 128 : half * 128 + 128], 0, 1)
                    for e in range(2)
                ]
                out_ref[o, half * 8 : half * 8 + 8, rows, :] = (
                    jnp.concatenate(parts, axis=1).astype(BF)
                )
        return carry

    lax.fori_loop(0, TILES // 2, project, 0)


def y_slopes():
    here = np.eye(128, dtype=np.float32)
    both = [np.kron(np.eye(2), np.roll(here, by, axis=1) - here) for by in (-1, 1)]
    return jnp.asarray(np.concatenate(both, axis=1), BF)


def evolve(ints, speeds, matrix, own, par):
    smem = pl.BlockSpec(memory_space=pltpu.SMEM)

    def stream(index):
        return pl.BlockSpec((32, None, 64, 128), lambda v: (0, index(v), 0, 0))

    def coef_array(planes=PLANES, tiles=TILES):
        return pltpu.VMEM((planes, tiles, 8, 256), BF)

    wide = jnp.kron(matrix, jnp.eye(32, dtype=jnp.float32)).astype(BF)
    return pl.pallas_call(
        evolve_kernel,
        name="evolve",
        grid=(VARS,),
        in_specs=[
            smem, smem, pl.BlockSpec((256, 256), lambda v: (0, 0)),
            pl.BlockSpec((256, 512), lambda v: (0, 0)),
            stream(lambda v: 0), stream(lambda v: 0), stream(lambda v: 6),
            stream(lambda v: v + 1), stream(lambda v: v + 1),
            stream(lambda v: jnp.minimum(v + 7, 8)), stream(lambda v: jnp.maximum(v + 4, 6)),
        ],
        out_specs=pl.BlockSpec((8, None, 16, 128, 128), lambda v: (0, v, 0, 0, 0)),
        out_shape=jax.ShapeDtypeStruct((8, VARS, 16, 128, 128), BF),
        scratch_shapes=[
            pltpu.VMEM((2, 8, 8, 8, 256), jnp.float32),
            pltpu.VMEM((14, TILES, 8, 512), BF),
            pltpu.VMEM((SNAPS, 8, TILES, 8, 256), BF),
            pltpu.VMEM((PLANES, TILES, 8, 256), jnp.float32),
            pltpu.VMEM((PLANES, TILES, 8, 256), jnp.float32),
            coef_array(tiles=TILES + 2), coef_array(tiles=TILES + 2), coef_array(tiles=TILES + 1),
            coef_array(), coef_array(), coef_array(PLANES + 1),
            coef_array(), coef_array(), coef_array(),
            coef_array(), coef_array(), coef_array(),
        ],
        compiler_params=pltpu.CompilerParams(vmem_limit_bytes=66_000_000),
        cost_estimate=pl.CostEstimate(
            flops=400_000_000_000, bytes_accessed=40_000_000, transcendentals=0
        ),
    )(ints, speeds, wide, y_slopes(), own, par, own, own, par, own, par)


def ring_shift(axis_of_core, by):
    pairs = []
    for core in range(2):
        for y in range(4):
            for x in range(4):
                to = ((y + by) % 4, x) if axis_of_core[core] == "y" else (y, (x + by) % 4)
                pairs.append((core * 16 + y * 4 + x, core * 16 + to[0] * 4 + to[1]))
    return lambda value: lax.ppermute(value, ("grp_1", "dev_1", "dev_2"), pairs)


def swap_cores(value):
    return lax.ppermute(value, "grp_1", [(0, 1), (1, 0)])


SIDE = 24


def local_kernel(
    ints, speeds, weights, fields, final_ref, corr_ref,
    qa, qb, nx, nzp, nzm, nyp, nym, diag, snap,
):
    low, high = ints[0], ints[1]
    row = lax.broadcasted_iota(jnp.int32, (SIDE, 128), 0)
    mask = ((row >= ints[2]) & (row < ints[3])).astype(jnp.float32)
    rates = [[0.5 * speeds[v * 3 + d] for d in range(3)] for v in range(VARS)]

    def up(value):
        return pltpu.roll(value, SIDE - 1, axis=0)

    def down(value):
        return pltpu.roll(value, 1, axis=0)

    def faces(x, carry):
        mid = fields[0, x]
        right = (mid + fields[0, x + 1]) * 0.5
        left = (mid + fields[0, x - 1]) * 0.5
        above = (mid + up(mid)) * 0.5
        below = (mid + down(mid)) * 0.5
        ahead = (mid + pltpu.roll(mid, 127, axis=1)) * 0.5
        behind = (mid + pltpu.roll(mid, 1, axis=1)) * 0.5
        nx[x + 1] = right
        nx[x] = left
        nzp[x], nzm[x], nyp[x], nym[x] = above, below, ahead, behind
        diag[x] = 1.0 - ((right + left) + (above + below) + (ahead + behind))
        return carry

    lax.fori_loop(1, SIDE - 1, faces, 0)
    for v in range(VARS):
        qa[v] = fields[v + 1]
        qb[v] = fields[v + 1]

    def step(t, src, dst):
        def one(x, carry):
            for v in range(VARS):
                hx, hz, hy = rates[v]
                mid = src[v, x]
                new = (
                    diag[x] * mid
                    + ((nx[x + 1] - hx) * src[v, x + 1] + (nx[x] + hx) * src[v, x - 1])
                    + ((nzp[x] - hz) * up(mid) + (nzm[x] + hz) * down(mid))
                    + (
                        (nyp[x] - hy) * pltpu.roll(mid, 127, axis=1)
                        + (nym[x] + hy) * pltpu.roll(mid, 1, axis=1)
                    )
                )
                dst[v, x] = new * mask
            return carry

        lax.fori_loop(jnp.maximum(t, low), jnp.minimum(SIDE - t, high), one, 0)
        for v in range(VARS):
            for x in range(8):
                snap[t - 1, v, x] = dst[v, 8 + x, 8:16, :].astype(BF).astype(jnp.float32)

    def two_steps(k, carry):
        step(2 * k + 1, qa, qb)
        step(2 * k + 2, qb, qa)
        return carry

    lax.fori_loop(0, SNAPS // 2, two_steps, 0)
    for v in range(VARS):
        for x in range(8):
            final_ref[v, x] = qa[v, 8 + x, 8:16, :]

    corr_ref[...] = jnp.zeros_like(corr_ref)

    def correlate(v, carry):
        weight = weights[v]
        sums = [jnp.zeros((8, 128), jnp.float32)] * len(PAIRS)
        for x in range(8):
            vals = [snap[t, v, x] for t in range(SNAPS)]
            for n, (a, b) in enumerate(PAIRS):
                sums[n] = sums[n] + vals[a] * vals[b]
        for n in range(len(PAIRS)):
            corr_ref[n] += weight * sums[n]
        return carry

    lax.fori_loop(0, VARS, correlate, 0)


def local_steps(ints, speeds, weights, fields):
    smem = pl.BlockSpec(memory_space=pltpu.SMEM)
    vmem = pl.BlockSpec(memory_space=pltpu.VMEM)
    cube = pltpu.VMEM((SIDE, SIDE, 128), jnp.float32)
    cubes = pltpu.VMEM((VARS, SIDE, SIDE, 128), jnp.float32)
    return pl.pallas_call(
        local_kernel,
        name="local",
        in_specs=[smem, smem, smem, vmem],
        out_specs=[vmem, vmem],
        out_shape=[
            jax.ShapeDtypeStruct((VARS, 8, 8, 128), jnp.float32),
            jax.ShapeDtypeStruct((len(PAIRS), 8, 128), jnp.float32),
        ],
        scratch_shapes=[
            cubes, cubes, pltpu.VMEM((SIDE + 1, SIDE, 128), jnp.float32),
            cube, cube, cube, cube, cube,
            pltpu.VMEM((SNAPS, VARS, 8, 8, 128), jnp.float32),
        ],
        compiler_params=pltpu.CompilerParams(vmem_limit_bytes=24_000_000),
        cost_estimate=pl.CostEstimate(
            flops=4_000_000_000, bytes_accessed=6_000_000, transcendentals=0
        ),
    )(ints, speeds, weights, fields)


def local_ints():
    own = lax.axis_index(DEV)
    grp = lax.axis_index(GRP)
    bounds = [
        jnp.where(own == 0, 8, 0),
        jnp.where(own == 31, 16, SIDE),
        jnp.where(grp == 0, 8, 0),
        jnp.where(grp == 3, 16, SIDE),
    ]
    return jnp.stack(bounds).astype(jnp.int32)


def ring_sum(value, axes):
    one, two, three = (
        lax.ppermute(value, axes, [(i, (i + by) % 4) for i in range(4)]) for by in (1, 2, 3)
    )
    return (value + two) + (one + three)


def communicate(initial_state, viscosity, speeds, energy_weights):
    fields = jnp.concatenate([viscosity[None], initial_state])
    state = fields.astype(BF).reshape(VARS + 1, 64, 128)
    near = lax.ppermute(state[:3], GRP, [(2, 1), (1, 2)])
    far = lax.ppermute(state[3:], GRP, [(2, 0), (1, 3)])
    block = jnp.concatenate([state, near + far])
    block, fields = lax.optimization_barrier((block, fields))
    other = lax.ppermute(block, "dev_0", [(0, 1), (1, 0)])
    third = lax.ppermute(fields, GRP, [(1, 2), (2, 1)])
    par = swap_cores(fields)

    odd = lax.axis_index("grp_1") == 1
    column = jnp.concatenate(
        [jnp.where(odd, par, third), fields, jnp.where(odd, third, par)], axis=2
    )
    pair = jnp.stack([block, other])
    column, _ = lax.optimization_barrier((column, pair))
    near_axis = [ring_shift(("y", "x"), by) for by in (-1, 2, 1)]
    first = jnp.stack([pair] + [shift(pair) for shift in near_axis])
    up = [(i, i + 1) for i in range(31)]
    before_x = lax.ppermute(column, DEV, up)
    after_x = lax.ppermute(column, DEV, [(b, a) for a, b in up])
    cube = jnp.concatenate([before_x, column, after_x], axis=1)

    forward, back = ring_shift(("x", "y"), 1), ring_shift(("x", "y"), -1)
    before, after = forward(first), back(first)
    cube, _ = lax.optimization_barrier((cube, first))
    final, corr = local_steps(local_ints(), speeds, energy_weights, cube)
    sums = jnp.sum(corr, axis=(1, 2)) / CELLS
    before, after, sums = lax.optimization_barrier((before, after, sums))
    half_before, half_after = forward(before[:2]), back(after[2:])
    sums = ring_sum(sums, "dev_2")
    half_before, half_after, sums = lax.optimization_barrier((half_before, half_after, sums))
    across = jnp.concatenate([half_before, half_after])
    own = jnp.stack([first, after, across, before]).reshape(32, 9, 64, 128)
    partner = swap_cores(own)
    sums = ring_sum(ring_sum(sums, "dev_1"), ("grp_0", "dev_0"))
    sums = sums + swap_cores(sums)
    return own, partner, final, sums


def layout_ints():
    h, c, l, y, x = (lax.axis_index(axis) for axis in GRP_DEV)
    d = jnp.arange(32)
    to_l, to_y, to_x = (d // 16 + l) % 2, (d // 4 - y) % 4, (d - x) % 4

    def slots(core):
        outer = jnp.where(core == 0, to_x, to_y)
        return outer * 8 + jnp.where(core == 0, to_y, to_x) * 2 + to_l

    inner = (h != c).astype(jnp.int32)
    par_base = jnp.where(c == 1, LOW, HIGH)
    scalars = [par_base, LOW + HIGH - par_base, inner]
    return jnp.concatenate([slots(c), slots(1 - c), jnp.stack(scalars)]).astype(jnp.int32)


def body(initial_state, viscosity, speeds, energy_weights, block_index, block_offset):
    speeds = speeds.reshape(-1)
    own, par, final, sums = communicate(initial_state, viscosity, speeds, energy_weights)
    order = [[PAIRS.index((min(a, b), max(a, b))) for b in range(SNAPS)] for a in range(SNAPS)]
    corr_matrix = sums[jnp.array(order)]
    coef = block_coefficients(block_index, block_offset)
    own_coef = lax.dynamic_slice_in_dim(coef, lax.axis_index(DEV) * 2, 2, 0)
    energy, matrix = mode_matrix(own_coef, corr_matrix)
    modes = evolve(layout_ints(), speeds, matrix.reshape(8, SNAPS), own, par)
    return final, modes.reshape(2, BLOCKS, 2, VARS, 256, 8, 128), energy


def solution(mesh):
    torus = Mesh(mesh.devices.reshape(2, 2, 2, 4, 4), GRP_DEV)
    in_specs = (P(None, DEV, GRP, None), P(DEV, GRP, None), P(), P(), P(), P())
    out_specs = (P(None, DEV, GRP, None), P(DEV, None, None, None, None, GRP, None), P(DEV))
    return jax.shard_map(body, mesh=torus, in_specs=in_specs, out_specs=out_specs, check_vma=False)
```
